32 devices in a mesh: rep: 4 (over x, core), fsdp: 8 (over z, y).
Axes of the slice: x: 2, y: 2, z: 4, core: 2. Of those that a mesh axis runs over, the one named last changes fastest.
Arguments:
- tokens: bfloat16 [4096, 2048], P(('rep', 'fsdp')), may hold values from -6 to 6
- out_grad: bfloat16 [4096, 2048], P(('rep', 'fsdp')), may hold values from -6 to 6
- w_qkv: bfloat16 [2048, 6144], P(('rep', 'fsdp')), may hold values from -0.13258252 to 0.13258252
- w_out: bfloat16 [2048, 2048], P(('rep', 'fsdp')), may hold values from -0.5 to 0.5
- router: bfloat16 [2048, 16], P(('rep', 'fsdp')), may hold values from -0.25 to 0.25
- gains: bfloat16 [4, 2048], P(None, ('rep', 'fsdp')), may hold values from 0.5 to 4.5
- experts: bfloat16 [1024, 16, 3, 2048], P('rep', 'fsdp'), may hold values from -0.1875 to 0.1875
- seg_ids: int32 [64, 64], P(('rep', 'fsdp')), may hold values from 0 to 2, never falling along the last dimension, each value on 1 to 32 neighbouring positions
- routes: int32 [4096, 8], P(('rep', 'fsdp')), may hold values from 0 to 15, all different within a row; in each aligned block of 64 rows (0 to 63, 64 to 127, ...) at most 40 rows name the same one
Outputs:
- layer_out: bfloat16 [4096, 2048], P(('rep', 'fsdp'))
- tokens_grad: float32 [4096, 2048], P(('rep', 'fsdp'))
- grad_qkv: float32 [2048, 6144], P(('rep', 'fsdp'))
- grad_wout: float32 [2048, 2048], P(('rep', 'fsdp'))
- grad_router: float32 [2048, 16], P(('rep', 'fsdp'))
- grad_gains: float32 [4, 2048], P(None, ('rep', 'fsdp'))
- grad_experts: float32 [1024, 16, 3, 2048], P('rep', 'fsdp')
The draws below stay inside these ranges and needn't reach their ends.
Inputs may be any that keep to these rules, and one draw needn't show every extreme that they name: `routes`: each token names 8 different experts; within the rows of one micro-batch of one device (aligned blocks of 64 rows) no expert is named by more than 40 rows, a bound that some block reaches. `seg_ids`: within each row the ids never fall and start at 0; each sequence has 1 to 32 tokens, one exactly that many.
All inputs are finite; a program needn't handle non-finite values.
Results may differ from the reference program's by a relative error of at most 0.013.
The reference program's roundings to bfloat16 on the way count: a program that leaves them out, or rounds other values in their place, can miss the bound.
Values may be sent and summed in bfloat16 or wider, within the bound.
No kernel may reach another device: no remote copies, remote signals or barrier semaphores. Data moves between devices by JAX's collectives and lax.ppermute only.
A program may use at most 384 MiB of HBM per device.

```python
import math
import jax
import jax.numpy as jnp
import numpy as np
from jax import lax

D = 2048
HEADS = 16
HEAD_DIM = 128
FF = 1024
TOP = 8
MB_TOK = 64
SEQS = 3
EXPERTS = 16
CAP = 40
TOKENS = 4096
BLOCKS = 64


def draw_w_qkv(key, part):
    first_key = jax.random.fold_in(key, 0)
    matrix = jnp.clip(jax.random.normal(first_key, (D, 3 * D), jnp.float32), -6.0, 6.0) * D ** (-0.5)
    return matrix.astype(jnp.bfloat16)


def draw_gains(key, part):
    base = jax.random.uniform(key, (4, D), jnp.float32, 0.5, 1.5)
    return base.astype(jnp.bfloat16)


def levels(own_key, dims, cuts, smallest, largest):
    level = 1.0
    for axis_at, parts in cuts:
        draws = jax.random.uniform(jax.random.fold_in(jax.random.fold_in(own_key, 6), axis_at), (parts,), jnp.float32, smallest / len(cuts), largest / len(cuts))
        level = level * jnp.repeat(jnp.exp(draws), dims[axis_at] // parts).reshape((-1,) + (1,) * (len(dims) - 1 - axis_at))
    return level


def profile(number_of, total, most, slope):
    weights = [(1 << 20) // math.isqrt(grade ** slope) + 1 for grade in range(2, number_of + 1)]
    spare, holding = total - most - (number_of - 1), [1] * (number_of - 1)
    while spare > 0:
        candidates = [i for i in range(number_of - 1) if holding[i] < most]
        whole, budget = sum([weights[i] for i in candidates]), spare
        for i in candidates:
            addition = min(most - holding[i], max(1, budget * weights[i] // whole), spare)
            holding[i] = holding[i] + addition
            spare = spare - addition
    return np.array([most] + holding)


def ragged(own_key, number_of, total, most, slope):
    if number_of == 2:
        one = jax.random.randint(own_key, (), max(1, total - most), min(most, total - 1) + 1)
        return jnp.stack([one, total - one])
    tallies = jnp.asarray(profile(number_of, total, most, slope), jnp.int32)
    pairs = (number_of - 1) // 2
    giver, taker = tallies[1:1 + 2 * pairs:2], tallies[2:2 + 2 * pairs:2]
    slack = jnp.minimum(giver - 1, most - taker)
    moved = jax.random.randint(jax.random.fold_in(own_key, 1), (pairs,), 0, 1 << 20) % (slack + 1)
    tallies = tallies.at[1:1 + 2 * pairs:2].set(giver - moved).at[2:2 + 2 * pairs:2].set(taker + moved)
    return tallies[jax.random.permutation(jax.random.fold_in(own_key, 2), number_of)]


def assign_block(stream_key, own, number, rows, count, top, most, skew):
    sequence = jax.random.permutation(stream_key, count)
    heavy_load, usual = load_shares(count, rows * top, most, skew, True), load_shares(count, rows * top, most, skew, False)
    places = jnp.arange(count)

    def named(tallies, offset_by):
        used = int((tallies > 0).sum())
        fixed = max(1, used // 4)
        moved = fixed + (places - fixed + offset_by * (used - fixed)) % max(1, count - fixed)
        return jnp.zeros((count,), jnp.int32).at[sequence[jnp.where(places < fixed, places, moved)]].set(jnp.asarray(tallies, jnp.int32))

    tallies = jnp.where(number % 4 == 0, named(heavy_load, number // 4), named(usual, number - number // 4 - 1))
    mixed = jax.random.permutation(jax.random.fold_in(own, 3), count)
    donor, sink = mixed[0:count // 2 * 2:2], mixed[1:count // 2 * 2:2]
    room = jnp.minimum(tallies[donor] - 1, most - tallies[sink]) // 2
    room = jnp.where((donor == sequence[0]) | (sink == sequence[0]) | (tallies[sink] == 0), 0, jnp.maximum(room, 0))
    moved = jax.random.randint(jax.random.fold_in(own, 4), (count // 2,), 0, 1 << 20) % (room + 1)
    tallies = tallies.at[donor].add(-moved).at[sink].add(moved)
    items = jnp.searchsorted(jnp.cumsum(tallies), jnp.arange(rows * top), side="right").astype(jnp.int32)
    table = items.reshape(top, rows).T
    table = table[jax.random.permutation(jax.random.fold_in(own, 1), rows)]
    offset_by = jax.random.randint(jax.random.fold_in(own, 2), (rows, 1), 0, top)
    return jnp.take_along_axis(table, (jnp.arange(top)[None, :] + offset_by) % top, axis=1)


def load_shares(amount, total, bound, skew, full):
    weights = [(1 << 20) // math.isqrt(standing ** skew) + 1 for standing in range(1, amount + 1)]
    largest = bound if full else min(bound, max(-(-total // amount), total * weights[0] // sum(weights)))
    least = 1 if total - largest >= amount - 1 else 0
    given, surplus = [largest] + [least] * (amount - 1), total - largest - least * (amount - 1)
    while surplus > 0:
        movable = [i for i in range(1, amount) if given[i] < largest] or [i for i in range(1, amount) if given[i] < bound]
        whole, budget = sum([weights[i] for i in movable]), surplus
        for i in movable:
            extra = min(bound - given[i], max(1, budget * weights[i] // whole), surplus)
            given[i] = given[i] + extra
            surplus = surplus - extra
    return np.array(given)


def noise(stream_key, dims, scale, reach, cuts=(), kind=jnp.bfloat16):
    gain = levels(stream_key, dims, cuts, -0.22, 0.18) if cuts else 1.0
    values = jax.random.normal(stream_key, dims, jnp.float32) * scale * gain
    return jnp.minimum(jnp.maximum(values, -reach), reach).astype(kind)


def setup_inputs(seed: int = 0) -> dict:
    splits = jax.random.split(jax.random.key(seed), 10)
    tokens = noise(splits[0], (TOKENS, D), 1.0, 6.0, ((0, 32),))
    out_grad = noise(splits[1], (TOKENS, D), 1.0, 6.0, ((0, 32),))
    w_qkv = draw_w_qkv(jax.random.fold_in(splits[9], 71), 0)
    w_out = noise(splits[3], (D, D), (D // 16) ** -0.5, 0.5, ((0, 32),))
    router = noise(splits[4], (D, EXPERTS), (D // 4) ** -0.5, 0.25, ((0, 32),))
    gains = draw_gains(jax.random.fold_in(splits[9], 71), 0)
    experts = noise(splits[6], (FF, EXPERTS, 3, D), (D // 2) ** -0.5, 0.1875, ((0, 4), (1, 8)))
    seg_ids = jax.vmap(lambda own: jnp.searchsorted(jnp.cumsum(ragged(own, SEQS, MB_TOK, MB_TOK // 2, 1)), jnp.arange(MB_TOK), side="right"))(jax.random.split(splits[7], BLOCKS)).reshape((BLOCKS, MB_TOK)).astype(jnp.int32)
    routes_keys = jax.random.split(jax.random.fold_in(splits[8], 1), TOKENS // MB_TOK)
    routes_turns = jax.random.permutation(jax.random.fold_in(splits[8], 3), TOKENS // MB_TOK)
    routes = jax.vmap(lambda own, number: assign_block(jax.random.fold_in(splits[8], 2), own, number, MB_TOK, EXPERTS, TOP, CAP, 1))(routes_keys, routes_turns).reshape((TOKENS, TOP))
    return {"tokens": tokens, "out_grad": out_grad, "w_qkv": w_qkv, "w_out": w_out, "router": router, "gains": gains, "experts": experts, "seg_ids": seg_ids, "routes": routes}


@jax.custom_vjp
def low(v):
    return lax.optimization_barrier(v.astype(jnp.bfloat16)).astype(jnp.float32)

@jax.custom_vjp
def low_back(v):
    return v

def low_keep(v):
    return (low(v), None)

def low_pass(kept, grad):
    return (grad,)

def back_keep(v):
    return (v, None)

def back_low(kept, grad):
    return (low(grad),)
low.defvjp(low_keep, low_pass)
low_back.defvjp(back_keep, back_low)
epsilon = 1e-05
rope_base = 10000.0
highest = lax.Precision.HIGHEST

def matmul(left_side, right_side):
    return jnp.dot(left_side, right_side, precision=highest, preferred_element_type=jnp.float32)

def matmul_nt(left_side, right_side):
    return lax.dot_general(left_side, right_side, (((1,), (1,)), ((), ())), precision=highest, preferred_element_type=jnp.float32)

def rms_scale(values):
    return lax.rsqrt(lax.optimization_barrier(jnp.mean(values * values, axis=-1, keepdims=True)) + epsilon)

def rotate_half(values):
    half_dim = values.shape[-1] // 2
    return jnp.concatenate([-values[..., half_dim:], values[..., :half_dim]], axis=-1)

def rope_tables(seg_rows):
    row_count = seg_rows.shape[-1]
    earlier_count = lax.optimization_barrier(jnp.sum((seg_rows[..., None, :] < seg_rows[..., :, None]).astype(jnp.int32), axis=-1))
    position = (jnp.arange(row_count, dtype=jnp.int32) - earlier_count).astype(jnp.float32)
    frequency = jnp.power(rope_base, -jnp.arange(HEAD_DIM // 2, dtype=jnp.float32) * 2.0 / HEAD_DIM)
    angles = position[..., None] * frequency
    angles = jnp.concatenate([angles, angles], axis=-1)
    return (jnp.cos(angles), jnp.sin(angles))

def causal_mask(seg_rows):
    row_count = seg_rows.shape[-1]
    row_order = jnp.arange(row_count, dtype=jnp.int32)
    same_seq = seg_rows[..., :, None] == seg_rows[..., None, :]
    return same_seq & (row_order[:, None] >= row_order[None, :])

def slot_positions(routes):
    blocks = routes.shape[0] // MB_TOK
    flat_routes = routes.reshape(blocks, MB_TOK * TOP)
    route_hits = (flat_routes[:, :, None] == jnp.arange(EXPERTS, dtype=jnp.int32)).astype(jnp.int32)
    before = jnp.cumsum(route_hits, axis=1) - route_hits
    return lax.optimization_barrier(jnp.sum(before * route_hits, axis=2))

def expert_block(pair_in):
    slot_rows, weight = pair_in
    gate = low_back(matmul_nt(slot_rows, weight[:, 0, :]))
    upward = low_back(matmul_nt(slot_rows, weight[:, 1, :]))
    active = low(jax.nn.silu(gate) * upward)
    return low_back(low(matmul(active, weight[:, 2, :])))

def forward(tokens, w_qkv, w_out, router, gains, experts, seg_ids, routes):
    blocks = TOKENS // MB_TOK
    rows_all = blocks * CAP
    scale_one = rms_scale(tokens)
    normed = low(tokens * scale_one * gains[0])
    qkv_rows = low_back(matmul(normed, w_qkv))
    q_raw = qkv_rows[:, :D]
    k_raw = qkv_rows[:, D:2 * D]
    v_raw = qkv_rows[:, 2 * D:]
    q_norm = q_raw * rms_scale(q_raw) * gains[1]
    k_norm = k_raw * rms_scale(k_raw) * gains[2]
    cosine, sine = rope_tables(seg_ids)
    cosine = cosine[:, :, None, :]
    sine = sine[:, :, None, :]

    def split_heads(values):
        return values.reshape(blocks, MB_TOK, HEADS, HEAD_DIM)
    queries = low(split_heads(q_norm) * cosine + rotate_half(split_heads(q_norm)) * sine)
    key_rot = low(split_heads(k_norm) * cosine + rotate_half(split_heads(k_norm)) * sine)
    values_h = low(split_heads(v_raw))
    scores = low_back(jnp.einsum('bqhd,bkhd->bhqk', queries, key_rot, precision=highest)) * HEAD_DIM ** (-0.5)
    allowed = causal_mask(seg_ids)[:, None]
    probs = jax.nn.softmax(jnp.where(allowed, scores, -1e+30), axis=-1)
    mixed_rows = jnp.einsum('bhqk,bkhd->bqhd', low(probs), values_h, precision=highest)
    attn_in = low_back(low(mixed_rows.reshape(TOKENS, D)))
    hidden = tokens + low_back(matmul(attn_in, w_out))
    scale_two = rms_scale(hidden)
    normed2 = low(hidden * scale_two * gains[3])
    logits = low_back(matmul(normed2, router))
    gate_probs = jax.nn.softmax(logits, axis=-1)
    chosen = jnp.take_along_axis(gate_probs, routes, axis=1)
    slots = slot_positions(routes)
    block_base = (jnp.arange(blocks, dtype=jnp.int32) * CAP)[:, None]
    target = (routes.reshape(blocks, MB_TOK * TOP) * rows_all + block_base + slots).reshape(-1)
    source = jnp.repeat(jnp.arange(TOKENS, dtype=jnp.int32), TOP)
    slot_table = jnp.full((EXPERTS * rows_all,), TOKENS, jnp.int32).at[target].set(source)
    padded = jnp.concatenate([normed2, jnp.zeros((1, D), normed2.dtype)], axis=0)
    slot_rows = low_back(padded[slot_table]).reshape(EXPERTS, rows_all, D)
    per_expert = jnp.moveaxis(experts, 1, 0)
    results = lax.map(jax.checkpoint(expert_block), (slot_rows, per_expert))
    flat_out = results.reshape(EXPERTS * rows_all, D)
    target_pairs = target.reshape(TOKENS, TOP)
    mixture = jnp.zeros_like(hidden)
    for slot_k in range(TOP):
        mixture = mixture + chosen[:, slot_k:slot_k + 1] * flat_out[target_pairs[:, slot_k]]
    return hidden + mixture

def reference(tokens, out_grad, w_qkv, w_out, router, gains, experts, seg_ids, routes):

    def layer(x_in, qkv_w, out_w, router_w, gain_w, expert_w):
        return forward(x_in, qkv_w, out_w, router_w, gain_w, expert_w, seg_ids, routes)
    result, pullback = jax.vjp(layer, tokens.astype(jnp.float32), w_qkv.astype(jnp.float32), w_out.astype(jnp.float32), router.astype(jnp.float32), gains.astype(jnp.float32), experts.astype(jnp.float32))
    gradients = pullback(out_grad.astype(jnp.float32))
    return (result.astype(jnp.bfloat16), gradients[0], gradients[1], gradients[2], gradients[3], gradients[4], gradients[5])
```

```python
import jax
import jax.numpy as jnp
from jax import lax
from jax.sharding import PartitionSpec as P

HEAD_DIM = 128
LANES = 128
GROUP = 4

epsilon = 1e-05
rope_base = 10000.0
bf16 = jnp.bfloat16
f32 = jnp.float32


def dot_plain(left_side, right_side):
    return jnp.dot(left_side, right_side, preferred_element_type=f32)


def dot_left_t(left_side, right_side):
    return lax.dot_general(
        left_side, right_side, (((0,), (0,)), ((), ())), preferred_element_type=f32
    )


def dot_right_t(left_side, right_side):
    return lax.dot_general(
        left_side, right_side, (((1,), (1,)), ((), ())), preferred_element_type=f32
    )


def rms_scale(values):
    return lax.rsqrt(jnp.mean(values * values, axis=-1, keepdims=True) + epsilon)


def rotate_half(values):
    half_dim = values.shape[-1] // 2
    return jnp.concatenate([-values[..., half_dim:], values[..., :half_dim]], axis=-1)


def rope_tables(seg_rows):
    row_count = seg_rows.shape[-1]
    earlier_count = jnp.sum(
        (seg_rows[..., None, :] < seg_rows[..., :, None]).astype(jnp.int32), axis=-1
    )
    position = (jnp.arange(row_count, dtype=jnp.int32) - earlier_count).astype(f32)
    frequency = jnp.power(rope_base, -jnp.arange(HEAD_DIM // 2, dtype=f32) * 2.0 / HEAD_DIM)
    angles = position[..., None] * frequency
    angles = jnp.concatenate([angles, angles], axis=-1)
    return (jnp.cos(angles), jnp.sin(angles))


def causal_mask(seg_rows):
    row_count = seg_rows.shape[-1]
    row_order = jnp.arange(row_count, dtype=jnp.int32)
    same_seq = seg_rows[..., :, None] == seg_rows[..., None, :]
    return same_seq & (row_order[:, None] >= row_order[None, :])


def norm_back(values, row_scale, gain_row, upstream):
    weighted = gain_row * upstream
    inner_sum = jnp.mean(weighted * values, axis=-1, keepdims=True)
    return row_scale * weighted - values * (row_scale * row_scale * row_scale) * inner_sum


def far(value):
    return lax.ppermute(value, "rep", [(i, i ^ 2) for i in range(4)])


def near(value):
    return lax.ppermute(value, "rep", [(i, i ^ 1) for i in range(4)])


def rep_gather(value):
    pair = jnp.stack([value, far(value)])
    other = near(pair)
    return jnp.stack([pair[0], other[0], pair[1], other[1]])


def rep_scatter_sum(parts):
    got = near(jnp.stack([parts[1], parts[3]]).astype(bf16)).astype(f32)
    kept = parts[0] + got[0]
    sent = far((parts[2] + got[1]).astype(bf16)).astype(f32)
    return kept + sent


def rep_total(parts):
    parts = parts + near(parts)[jnp.array([1, 0, 3, 2])]
    return parts + far(parts)[jnp.array([2, 3, 0, 1])]


def by_rep(parts, index):
    return jnp.stack(
        [lax.dynamic_index_in_dim(parts, index ^ i, 0, keepdims=False) for i in range(4)]
    )


def fsdp_gather(value, axis=0):
    return lax.all_gather(value, "fsdp", axis=axis, tiled=True)


def fsdp_scatter_sum(value, axis=0):
    return lax.psum_scatter(value, "fsdp", scatter_dimension=axis, tiled=True)


def per_device(tokens, out_grad, w_qkv, w_out, router, gains, experts, seg_ids, routes):
    block_len = seg_ids.shape[1]
    rows_dev, width = tokens.shape
    n_exp = router.shape[1]
    exp_dev = experts.shape[1]
    top_count = routes.shape[1]
    n_fsdp = lax.axis_size("fsdp")
    rep_at = lax.axis_index("rep")
    fsdp_at = lax.axis_index("fsdp")
    capacity = max(2, block_len * top_count * 5 // (4 * n_exp))
    att_scale = HEAD_DIM ** (-0.5)
    shard = w_qkv.shape[0]
    part = width // 4
    heads = part // HEAD_DIM
    group_rows = 4 * rows_dev
    n_blocks = group_rows // block_len
    total_rows = n_fsdp * rows_dev

    e_far = far(experts)
    e_near = near(jnp.stack([experts, e_far]))
    e_parts = [experts, e_near[0], e_far, e_near[1]]

    tok_ext = jnp.concatenate(
        [tokens, jnp.pad(seg_ids.reshape(rows_dev, 1), ((0, 0), (0, LANES - 1))).astype(bf16)],
        axis=1,
    )
    tok_all = rep_gather(tok_ext).reshape(group_rows, width + LANES)
    inputs_all = tok_all[:, :width].astype(f32)
    seg_all = tok_all[:, width].astype(jnp.int32).reshape(n_blocks, block_len)
    inputs = tokens.astype(f32)
    upstream = out_grad.astype(f32)

    columns = w_qkv.reshape(shard, 3, 4, part)

    def column_group(q):
        return lax.dynamic_index_in_dim(columns, rep_at ^ q, 2, keepdims=False).reshape(
            shard, 3 * part
        )

    got = far(jnp.stack([column_group(2), column_group(3)]))
    got2 = near(jnp.stack([column_group(1), got[1]]))
    w_rows = by_rep(jnp.stack([column_group(0), got2[0], got[0], got2[1]]), rep_at)
    small = jnp.concatenate(
        [router, gains.T, jnp.zeros((shard, LANES - (n_exp + 4) % LANES), bf16)], axis=1
    )
    small_cols = small.shape[1]
    small_rows = by_rep(rep_gather(small), rep_at)
    w_full = fsdp_gather(jnp.concatenate([w_rows, small_rows], axis=2), axis=1).reshape(
        width, 3 * part + small_cols
    )
    w_heads = w_full[:, : 3 * part]
    full_router = w_full[:, 3 * part : 3 * part + n_exp]
    gain_f = w_full[:, 3 * part + n_exp : 3 * part + n_exp + 4].astype(f32).T
    o_heads = fsdp_gather(w_out)
    gain_q = lax.dynamic_slice_in_dim(gain_f[1], rep_at * part, part, 0)
    gain_k = lax.dynamic_slice_in_dim(gain_f[2], rep_at * part, part, 0)

    g_ext = jnp.concatenate(
        [out_grad, jnp.pad(routes, ((0, 0), (0, LANES - top_count))).astype(bf16)], axis=1
    )
    g_all = fsdp_gather(g_ext)

    scale_one_all = rms_scale(inputs_all)
    normed_all = (inputs_all * scale_one_all * gain_f[0]).astype(bf16)
    qkv_rows = dot_plain(normed_all, w_heads)
    q_raw = qkv_rows[:, :part]
    k_raw = qkv_rows[:, part : 2 * part]
    v_raw = qkv_rows[:, 2 * part :]
    squares = jnp.stack([jnp.sum(q_raw * q_raw, axis=1), jnp.sum(k_raw * k_raw, axis=1)])
    squares = rep_total(squares.reshape(2, 4, rows_dev).transpose(1, 0, 2))
    squares = squares.transpose(1, 0, 2).reshape(2, group_rows, 1)
    q_scale = lax.rsqrt(squares[0] / width + epsilon)
    k_scale = lax.rsqrt(squares[1] / width + epsilon)
    shape4 = (n_blocks, block_len, heads, HEAD_DIM)
    q_norm = (q_raw * q_scale * gain_q).reshape(shape4)
    k_norm = (k_raw * k_scale * gain_k).reshape(shape4)
    cosine, sine = rope_tables(seg_all)
    cosine = cosine[:, :, None, :]
    sine = sine[:, :, None, :]
    queries = (q_norm * cosine + rotate_half(q_norm) * sine).astype(bf16)
    key_rot = (k_norm * cosine + rotate_half(k_norm) * sine).astype(bf16)
    values_h = v_raw.reshape(shape4).astype(bf16)
    allowed = causal_mask(seg_all)[:, None]
    scores = (
        jnp.einsum("bqhd,bkhd->bhqk", queries, key_rot, preferred_element_type=f32) * att_scale
    )
    masked = jnp.where(allowed, scores, -1e30)
    top_score = jnp.max(masked, axis=-1, keepdims=True)
    expd = jnp.exp(masked - top_score)
    totals = jnp.sum(expd, axis=-1, keepdims=True)
    probs = expd / totals
    probs_low = probs.astype(bf16)
    mixed_rows = (
        jnp.einsum("bhqk,bkhd->bqhd", probs_low, values_h, preferred_element_type=f32)
        .reshape(group_rows, part)
        .astype(bf16)
    )
    out_parts = dot_plain(mixed_rows, o_heads).reshape(4, rows_dev, width)
    hidden = inputs + rep_scatter_sum(out_parts)
    scale_two = rms_scale(hidden)
    normed2 = (hidden * scale_two * gain_f[3]).astype(bf16)

    n2_all = fsdp_gather(normed2)
    up_all = g_all[:, :width]
    route_all = g_all[:, width : width + top_count].astype(jnp.int32)
    probs_all = jax.nn.softmax(dot_plain(n2_all, full_router), axis=-1)
    own_probs = lax.dynamic_slice_in_dim(probs_all, fsdp_at * exp_dev, exp_dev, 1)
    own_ids = fsdp_at * exp_dev + jnp.arange(exp_dev, dtype=jnp.int32)
    hits = jnp.any(route_all[:, :, None] == own_ids, axis=1)
    block_hits = hits.astype(bf16).reshape(total_rows // block_len, block_len, exp_dev)
    order = jnp.arange(block_len, dtype=jnp.int32)
    earlier = (order[:, None] > order[None, :]).astype(bf16)
    prior = jnp.einsum("tu,buj->btj", earlier, block_hits, preferred_element_type=f32)
    in_group = (jnp.arange(total_rows, dtype=jnp.int32) // block_len) % GROUP
    slot = in_group[:, None] * capacity + prior.astype(jnp.int32).reshape(total_rows, exp_dev)
    slot = jnp.where(hits, slot, -1)
    n_groups = total_rows // (GROUP * block_len)
    slots = slot.reshape(n_groups, GROUP * block_len, exp_dev).transpose(0, 2, 1)
    slot_ids = jnp.arange(GROUP * capacity, dtype=jnp.int32)
    pick = (slots[:, :, None, :] == slot_ids[:, None]).astype(bf16)
    exp_rows = n_groups * GROUP * capacity
    n2_groups = n2_all.reshape(n_groups, GROUP * block_len, width)
    rows_in = (
        jnp.einsum("gjst,gtd->jgsd", pick, n2_groups, preferred_element_type=f32)
        .astype(bf16)
        .reshape(exp_dev, exp_rows, width)
    )
    weighted_up = (own_probs.T[:, :, None] * up_all.astype(f32)).astype(bf16)
    rows_up = (
        jnp.einsum(
            "gjst,jgtd->jgsd",
            pick,
            weighted_up.reshape(exp_dev, n_groups, GROUP * block_len, width),
            preferred_element_type=f32,
        )
        .astype(bf16)
        .reshape(exp_dev, exp_rows, width)
    )
    out_sum = jnp.zeros((exp_dev, exp_rows, width), f32)
    back_sum = jnp.zeros((exp_dev, exp_rows, width), f32)
    e_grads = []
    for e_part in e_parts:
        pre_act = jnp.einsum(
            "jsd,fjgd->gjsf", rows_in, e_part[:, :, 0:2, :], preferred_element_type=f32
        )
        gate_pre = pre_act[0]
        up_pre = pre_act[1]
        sig_gate = jax.nn.sigmoid(gate_pre)
        active = (gate_pre * sig_gate * up_pre).astype(bf16)
        out_sum = out_sum + jnp.einsum(
            "jsf,fjd->jsd", active, e_part[:, :, 2, :], preferred_element_type=f32
        )
        active_grad = jnp.einsum(
            "jsd,fjd->jsf", rows_up, e_part[:, :, 2, :], preferred_element_type=f32
        )
        up_bar = active_grad * (gate_pre * sig_gate)
        gate_bar = active_grad * up_pre * sig_gate * (1.0 + gate_pre * (1.0 - sig_gate))
        pre_grad = jnp.stack([gate_bar, up_bar]).astype(bf16)
        back_sum = back_sum + jnp.einsum(
            "gjsf,fjgd->jsd", pre_grad, e_part[:, :, 0:2, :], preferred_element_type=f32
        )
        pair_term = jnp.einsum("gjsf,jsd->fjgd", pre_grad, rows_in, preferred_element_type=f32)
        down_term = jnp.einsum("jsf,jsd->fjd", active, rows_up, preferred_element_type=f32)
        e_grads.append(jnp.concatenate([pair_term, down_term[:, :, None, :]], axis=2))
    produced = out_sum.astype(bf16).reshape(exp_dev, n_groups, GROUP * capacity, width)
    rows_grad = back_sum.astype(bf16).reshape(exp_dev, n_groups, GROUP * capacity, width)

    e_got = near(jnp.stack([e_grads[1], e_grads[3]]).astype(bf16)).astype(f32)
    e_sent = far((e_grads[2] + e_got[1]).astype(bf16)).astype(f32)
    expert_grad = e_grads[0] + e_got[0] + e_sent

    picked = jnp.einsum("gjst,jgsd->jgtd", pick, produced, preferred_element_type=f32).reshape(
        exp_dev, total_rows, width
    )
    mix_part = jnp.sum(own_probs.T[:, :, None] * picked, axis=0)
    prob_part = jnp.sum(picked * up_all.astype(f32), axis=-1).T
    prob_cols = lax.dynamic_update_slice(
        jnp.zeros((total_rows, n_exp), f32), prob_part, (0, fsdp_at * exp_dev)
    )
    prob_high = prob_cols.astype(bf16)
    prob_low = (prob_cols - prob_high.astype(f32)).astype(bf16)
    prob_pad = jnp.zeros((total_rows, -(2 * n_exp) % LANES), bf16)
    mix_ext = jnp.concatenate([mix_part.astype(bf16), prob_high, prob_low, prob_pad], axis=1)
    mix_got = fsdp_scatter_sum(mix_ext)
    layer_out = (hidden + mix_got[:, :width].astype(f32)).astype(bf16)
    prob_grad = mix_got[:, width : width + n_exp].astype(f32) + mix_got[
        :, width + n_exp : width + 2 * n_exp
    ].astype(f32)
    back_part = jnp.einsum("gjst,jgsd->gtd", pick, rows_grad, preferred_element_type=f32)
    input_grad = fsdp_scatter_sum(back_part.astype(bf16).reshape(total_rows, width)).astype(f32)

    gate_probs = jax.nn.softmax(dot_plain(normed2, full_router), axis=-1)
    logit_grad = (
        gate_probs * (prob_grad - jnp.sum(prob_grad * gate_probs, axis=-1, keepdims=True))
    ).astype(bf16)
    normed2_grad = dot_right_t(logit_grad, full_router) + input_grad
    hidden_grad = upstream + norm_back(hidden, scale_two, gain_f[3], normed2_grad)
    gain_three = jnp.sum(normed2_grad * hidden * scale_two, axis=0)
    router_part = dot_left_t(normed2, logit_grad)

    attn_grad = rep_gather(hidden_grad.astype(bf16)).reshape(group_rows, width)
    mixed_grad = dot_right_t(attn_grad, o_heads).astype(bf16)
    mixed_grad4 = mixed_grad.reshape(shape4)
    weight_grad = jnp.einsum("bqhd,bkhd->bhqk", mixed_grad4, values_h, preferred_element_type=f32)
    inner_sum = jnp.sum(probs * weight_grad, axis=-1, keepdims=True)
    score_grad = (probs * (weight_grad - inner_sum) * att_scale).astype(bf16)
    query_grad = jnp.einsum("bhqk,bkhd->bqhd", score_grad, key_rot, preferred_element_type=f32)
    key_grad = jnp.einsum("bhqk,bqhd->bkhd", score_grad, queries, preferred_element_type=f32)
    value_grad = jnp.einsum("bhqk,bqhd->bkhd", probs_low, mixed_grad4, preferred_element_type=f32)
    qn_grad = (query_grad * cosine - rotate_half(query_grad * sine)).reshape(group_rows, part)
    kn_grad = (key_grad * cosine - rotate_half(key_grad * sine)).reshape(group_rows, part)
    q_gain = qn_grad * q_raw
    k_gain = kn_grad * k_raw
    inner = jnp.stack([jnp.sum(q_gain * gain_q, axis=1), jnp.sum(k_gain * gain_k, axis=1)])
    inner = rep_total(inner.reshape(2, 4, rows_dev).transpose(1, 0, 2))
    inner = inner.transpose(1, 0, 2).reshape(2, group_rows, 1) / width
    gain_one = jnp.sum(q_gain * q_scale, axis=0)
    gain_two = jnp.sum(k_gain * k_scale, axis=0)
    q_part = q_scale * (gain_q * qn_grad) - q_raw * (q_scale * q_scale * q_scale) * inner[0]
    k_part = k_scale * (gain_k * kn_grad) - k_raw * (k_scale * k_scale * k_scale) * inner[1]
    qkv_grad = jnp.concatenate(
        [q_part, k_part, value_grad.reshape(group_rows, part)], axis=1
    ).astype(bf16)
    normed_grad = rep_scatter_sum(dot_right_t(qkv_grad, w_heads).reshape(4, rows_dev, width))
    scale_one = rms_scale(inputs)
    tokens_grad = hidden_grad + norm_back(inputs, scale_one, gain_f[0], normed_grad)
    gain_zero = jnp.sum(normed_grad * inputs * scale_one, axis=0)

    gain_rows = jnp.stack(
        [
            gain_zero,
            lax.dynamic_update_slice(jnp.zeros((width,), f32), gain_one, (rep_at * part,)),
            lax.dynamic_update_slice(jnp.zeros((width,), f32), gain_two, (rep_at * part,)),
            gain_three,
        ]
    )
    small_grad = jnp.concatenate(
        [router_part, gain_rows.T, jnp.zeros((width, small_cols - n_exp - 4), f32)], axis=1
    )
    w_grad = jnp.concatenate([dot_left_t(normed_all, qkv_grad), small_grad], axis=1)
    w_got = fsdp_scatter_sum(
        w_grad.astype(bf16).reshape(4, n_fsdp * shard, 3 * part + small_cols), axis=1
    )
    rel = by_rep(w_got, rep_at)
    pair_far = far(jnp.stack([rel[2], rel[3]]))
    pair_near = near(jnp.stack([rel[1], pair_far[1]]))
    col_groups = by_rep(
        jnp.stack([rel[0], pair_near[0], pair_far[0], pair_near[1]])[:, :, : 3 * part], rep_at
    )
    grad_qkv = (
        col_groups.reshape(4, shard, 3, part)
        .transpose(1, 2, 0, 3)
        .reshape(shard, 12 * part)
        .astype(f32)
    )
    small_got = (
        rel[0][:, 3 * part :].astype(f32)
        + pair_near[0][:, 3 * part :].astype(f32)
        + pair_far[0][:, 3 * part :].astype(f32)
        + pair_near[1][:, 3 * part :].astype(f32)
    )
    grad_wout = fsdp_scatter_sum(dot_left_t(mixed_rows, attn_grad).astype(bf16)).astype(f32)
    return (
        layer_out,
        tokens_grad,
        grad_qkv,
        grad_wout,
        small_got[:, :n_exp],
        small_got[:, n_exp : n_exp + 4].T,
        expert_grad,
    )


def solution(mesh):
    in_specs = (
        P(("rep", "fsdp"), None),
        P(("rep", "fsdp"), None),
        P(("rep", "fsdp"), None),
        P(("rep", "fsdp"), None),
        P(("rep", "fsdp"), None),
        P(None, ("rep", "fsdp")),
        P("rep", "fsdp", None, None),
        P(("rep", "fsdp"), None),
        P(("rep", "fsdp"), None),
    )
    out_specs = (
        P(("rep", "fsdp"), None),
        P(("rep", "fsdp"), None),
        P(("rep", "fsdp"), None),
        P(("rep", "fsdp"), None),
        P(("rep", "fsdp"), None),
        P(None, ("rep", "fsdp")),
        P("rep", "fsdp", None, None),
    )
    return jax.shard_map(
        per_device, mesh=mesh, in_specs=in_specs, out_specs=out_specs, check_vma=False
    )
```

```python
import functools

import jax
import jax.numpy as jnp
from jax import lax
from jax.experimental import pallas as pl
from jax.experimental.pallas import tpu as pltpu
from jax.sharding import PartitionSpec as P

HEAD_DIM = 128
LANES = 128
GROUP = 4
TOP_LANES = 8

epsilon = 1e-05
rope_base = 10000.0
bf16 = jnp.bfloat16
f32 = jnp.float32


def dot_plain(left_side, right_side):
    return jnp.dot(left_side, right_side, preferred_element_type=f32)


def dot_left_t(left_side, right_side):
    return lax.dot_general(
        left_side, right_side, (((0,), (0,)), ((), ())), preferred_element_type=f32
    )


def dot_right_t(left_side, right_side):
    return lax.dot_general(
        left_side, right_side, (((1,), (1,)), ((), ())), preferred_element_type=f32
    )


def rms_scale(values):
    return lax.rsqrt(jnp.mean(values * values, axis=-1, keepdims=True) + epsilon)


def rotate_half(values):
    half_dim = values.shape[-1] // 2
    return jnp.concatenate([-values[..., half_dim:], values[..., :half_dim]], axis=-1)


def rope_tables(seg_rows):
    row_count = seg_rows.shape[-1]
    earlier_count = jnp.sum(
        (seg_rows[..., None, :] < seg_rows[..., :, None]).astype(jnp.int32), axis=-1
    )
    position = (jnp.arange(row_count, dtype=jnp.int32) - earlier_count).astype(f32)
    frequency = jnp.power(rope_base, -jnp.arange(HEAD_DIM // 2, dtype=f32) * 2.0 / HEAD_DIM)
    angles = position[..., None] * frequency
    angles = jnp.concatenate([angles, angles], axis=-1)
    return (jnp.cos(angles), jnp.sin(angles))


def causal_mask(seg_rows):
    row_count = seg_rows.shape[-1]
    row_order = jnp.arange(row_count, dtype=jnp.int32)
    same_seq = seg_rows[..., :, None] == seg_rows[..., None, :]
    return same_seq & (row_order[:, None] >= row_order[None, :])


def norm_back(values, row_scale, gain_row, upstream):
    weighted = gain_row * upstream
    inner_sum = jnp.mean(weighted * values, axis=-1, keepdims=True)
    return row_scale * weighted - values * (row_scale * row_scale * row_scale) * inner_sum


def far(value):
    return lax.ppermute(value, "rep", [(i, i ^ 2) for i in range(4)])


def near(value):
    return lax.ppermute(value, "rep", [(i, i ^ 1) for i in range(4)])


def rep_gather(value):
    pair = jnp.stack([value, far(value)])
    other = near(pair)
    return jnp.stack([pair[0], other[0], pair[1], other[1]])


def rep_scatter_sum(parts):
    got = near(jnp.stack([parts[1], parts[3]]).astype(bf16)).astype(f32)
    kept = parts[0] + got[0]
    sent = far((parts[2] + got[1]).astype(bf16)).astype(f32)
    return kept + sent


def rep_total(parts):
    parts = parts + near(parts)[jnp.array([1, 0, 3, 2])]
    return parts + far(parts)[jnp.array([2, 3, 0, 1])]


def by_rep(parts, index):
    return jnp.stack(
        [lax.dynamic_index_in_dim(parts, index ^ i, 0, keepdims=False) for i in range(4)]
    )


def fsdp_gather(value, axis=0):
    return lax.all_gather(value, "fsdp", axis=axis, tiled=True)


def fsdp_scatter_sum(value, axis=0):
    return lax.psum_scatter(value, "fsdp", scatter_dimension=axis, tiled=True)


def cost(flops, bytes_accessed):
    return pl.CostEstimate(flops=flops, bytes_accessed=bytes_accessed, transcendentals=0)


def params(semantics):
    return pltpu.CompilerParams(
        dimension_semantics=("arbitrary",) * semantics, vmem_limit_bytes=60 << 20
    )


def pick_matrix(slot_column, slot_count):
    ids = lax.broadcasted_iota(jnp.int32, (slot_column.shape[0], slot_count), 1).astype(f32)
    return jnp.where(slot_column == ids, 1.0, 0.0).astype(bf16)


def dispatch_kernel(
    fsdp_ref, n2_ref, ext_ref, router_ref, x_ref, up_ref, aux_ref, *, n_exp, capacity, block_len
):
    rows, width = n2_ref.shape
    exp_dev = x_ref.shape[0]
    first = fsdp_ref[0] * exp_dev
    normed2 = n2_ref[...]
    lanes = lax.broadcasted_iota(jnp.int32, (rows, LANES), 1)
    logits = jnp.where(lanes < n_exp, dot_plain(normed2, router_ref[...]), -1e30)
    expd = jnp.exp(logits - jnp.max(logits, axis=1, keepdims=True))
    probs = expd / jnp.sum(expd, axis=1, keepdims=True)
    tail = ext_ref[:, width:].astype(f32)
    upstream = ext_ref[:, :width].astype(f32)
    at_row = lax.broadcasted_iota(jnp.int32, (rows, rows), 0)
    at_col = lax.broadcasted_iota(jnp.int32, (rows, rows), 1)
    earlier = jnp.where(
        (at_row // block_len == at_col // block_len) & (at_col < at_row), 1.0, 0.0
    ).astype(bf16)
    named = [
        jnp.max(
            jnp.where((tail == (first + j).astype(f32)) & (lanes < TOP_LANES), 1.0, 0.0),
            axis=1,
            keepdims=True,
        )
        for j in range(exp_dev)
    ]
    hit_lanes = jnp.zeros((rows, LANES), f32)
    for j in range(exp_dev):
        hit_lanes = jnp.where(lanes == j, named[j], hit_lanes)
    prior = dot_plain(earlier, hit_lanes.astype(bf16))
    base = (lax.broadcasted_iota(jnp.int32, (rows, 1), 0) // block_len * capacity).astype(f32)
    aux = jnp.zeros((rows, LANES), f32)
    for j in range(exp_dev):
        chosen = jnp.sum(jnp.where(lanes == first + j, probs, 0.0), axis=1, keepdims=True)
        slot = jnp.where(named[j] > 0.5, prior[:, j : j + 1] + base, -1.0)
        pick = pick_matrix(slot, x_ref.shape[2])
        x_ref[j, 0] = dot_left_t(pick, normed2).astype(bf16)
        up_ref[j, 0] = dot_left_t(pick, (chosen * upstream).astype(bf16)).astype(bf16)
        aux = jnp.where(lanes == j, chosen, aux)
        aux = jnp.where(lanes == exp_dev + j, slot, aux)
    aux_ref[...] = aux


def dispatch(fsdp_at, n2_all, g_all, small_full, n_exp, exp_dev, capacity, block_len):
    total_rows, width = n2_all.shape
    rows = GROUP * block_len
    n_groups = total_rows // rows
    slots = GROUP * capacity
    slot_spec = pl.BlockSpec((exp_dev, 1, slots, width), lambda i, s: (0, i, 0, 0))
    slot_shape = jax.ShapeDtypeStruct((exp_dev, n_groups, slots, width), bf16)
    return pl.pallas_call(
        functools.partial(
            dispatch_kernel, n_exp=n_exp, capacity=capacity, block_len=block_len
        ),
        grid_spec=pltpu.PrefetchScalarGridSpec(
            num_scalar_prefetch=1,
            grid=(n_groups,),
            in_specs=[
                pl.BlockSpec((rows, width), lambda i, s: (i, 0)),
                pl.BlockSpec((rows, g_all.shape[1]), lambda i, s: (i, 0)),
                pl.BlockSpec((width, LANES), lambda i, s: (0, 0)),
            ],
            out_specs=[slot_spec, slot_spec, pl.BlockSpec((rows, LANES), lambda i, s: (i, 0))],
        ),
        out_shape=[slot_shape, slot_shape, jax.ShapeDtypeStruct((total_rows, LANES), f32)],
        compiler_params=params(1),
        cost_estimate=cost(
            4 * exp_dev * total_rows * slots * width, 4 * total_rows * width * (2 + exp_dev)
        ),
        name="dispatch",
    )(fsdp_at.reshape(1), n2_all, g_all, small_full)


def ffn_kernel(
    x_ref, up_ref, e0, e1, e2, e3, out_ref, back_ref, act_ref, bar_ref,
    weights, out_acc, back_acc, sems,
):
    j = pl.program_id(0)
    t = pl.program_id(1)
    step = j * 4 + t
    parts = (e0, e1, e2, e3)

    def fetch(at_j, at_t, slot, go):
        for q, part in enumerate(parts):

            @pl.when(at_t == q)
            def _():
                copy = pltpu.make_async_copy(part.at[at_j], weights.at[slot], sems.at[slot])
                copy.start() if go else copy.wait()

    @pl.when(step == 0)
    def _():
        fetch(j, t, 0, True)

    @pl.when(step + 1 < 4 * pl.num_programs(0))
    def _():
        following = step + 1
        fetch(following // 4, following % 4, following % 2, True)

    fetch(j, t, step % 2, False)
    slot = step % 2
    hidden = weights.shape[2]
    width = x_ref.shape[2]
    pair = weights[slot, 0:2].reshape(2 * hidden, width)
    down = weights[slot, 2]
    pre = dot_right_t(x_ref[0], pair)
    gate_pre = pre[:, :hidden]
    up_pre = pre[:, hidden:]
    sig = jax.nn.sigmoid(gate_pre)
    active = (gate_pre * sig * up_pre).astype(bf16)
    act_ref[0, 0] = active
    grad = dot_right_t(up_ref[0], down)
    up_bar = grad * (gate_pre * sig)
    gate_bar = grad * up_pre * sig * (1.0 + gate_pre * (1.0 - sig))
    bar_ref[0, 0, :, :hidden] = gate_bar.astype(bf16)
    bar_ref[0, 0, :, hidden:] = up_bar.astype(bf16)

    @pl.when(t == 0)
    def _():
        out_acc[...] = dot_plain(active, down)
        back_acc[...] = dot_plain(bar_ref[0, 0], pair)

    @pl.when(t > 0)
    def _():
        out_acc[...] += dot_plain(active, down)
        back_acc[...] += dot_plain(bar_ref[0, 0], pair)

    @pl.when(t == 3)
    def _():
        out_ref[0] = out_acc[...].astype(bf16)
        back_ref[0] = back_acc[...].astype(bf16)


def ffn(rows_in, rows_up, e_parts):
    exp_dev, rows, width = rows_in.shape
    hidden = e_parts[0].shape[2]
    row_spec = pl.BlockSpec((1, rows, width), lambda j, t: (j, 0, 0))
    row_shape = jax.ShapeDtypeStruct((exp_dev, rows, width), bf16)
    return pl.pallas_call(
        ffn_kernel,
        grid=(exp_dev, 4),
        in_specs=[row_spec, row_spec] + [pl.BlockSpec(memory_space=pl.ANY)] * 4,
        out_specs=[
            row_spec,
            row_spec,
            pl.BlockSpec((1, 1, rows, hidden), lambda j, t: (j, t, 0, 0)),
            pl.BlockSpec((1, 1, rows, 2 * hidden), lambda j, t: (j, t, 0, 0)),
        ],
        out_shape=[
            row_shape,
            row_shape,
            jax.ShapeDtypeStruct((exp_dev, 4, rows, hidden), bf16),
            jax.ShapeDtypeStruct((exp_dev, 4, rows, 2 * hidden), bf16),
        ],
        scratch_shapes=[
            pltpu.VMEM((2, 3, hidden, width), bf16),
            pltpu.VMEM((rows, width), f32),
            pltpu.VMEM((rows, width), f32),
            pltpu.SemaphoreType.DMA((2,)),
        ],
        compiler_params=params(2),
        cost_estimate=cost(
            2 * exp_dev * rows * width * hidden * 4 * 6,
            2 * exp_dev * (4 * rows * width + 12 * hidden * (width + rows)),
        ),
        name="ffn",
    )(rows_in, rows_up, *e_parts)


def ffn_grad_kernel(x_ref, up_ref, act_ref, bar_ref, near_ref, own_ref):
    t = pl.program_id(1)
    hidden = act_ref.shape[3]

    def write(ref):
        pair = dot_left_t(bar_ref[0, 0], x_ref[0]).astype(bf16)
        ref[0, 0, 0] = pair[:hidden]
        ref[0, 0, 1] = pair[hidden:]
        ref[0, 0, 2] = dot_left_t(act_ref[0, 0], up_ref[0]).astype(bf16)

    @pl.when(t < 2)
    def _():
        write(near_ref)

    @pl.when(t >= 2)
    def _():
        write(own_ref)


def ffn_grad(rows_in, rows_up, active, bars):
    exp_dev, rows, width = rows_in.shape
    hidden = active.shape[3]
    row_spec = pl.BlockSpec((1, rows, width), lambda j, t: (j, 0, 0))

    def part_of(t):
        return jnp.where(t < 2, 2 * t + 1, 2 * t - 4)

    out_shape = jax.ShapeDtypeStruct((2, exp_dev, 3, hidden, width), bf16)
    block = (1, 1, 3, hidden, width)
    return pl.pallas_call(
        ffn_grad_kernel,
        grid=(exp_dev, 4),
        in_specs=[
            row_spec,
            row_spec,
            pl.BlockSpec((1, 1, rows, hidden), lambda j, t: (j, part_of(t), 0, 0)),
            pl.BlockSpec((1, 1, rows, 2 * hidden), lambda j, t: (j, part_of(t), 0, 0)),
        ],
        out_specs=[
            pl.BlockSpec(block, lambda j, t: (jnp.minimum(t, 1), j, 0, 0, 0)),
            pl.BlockSpec(block, lambda j, t: (jnp.maximum(t - 2, 0), j, 0, 0, 0)),
        ],
        out_shape=[out_shape, out_shape],
        compiler_params=params(2),
        cost_estimate=cost(
            2 * exp_dev * rows * width * hidden * 4 * 3,
            2 * exp_dev * (2 * rows * width + 12 * hidden * (width + rows)),
        ),
        name="ffn_grad",
    )(rows_in, rows_up, active, bars)


def combine_kernel(fsdp_ref, out_ref, rows_ref, aux_ref, g_ref, back_ref, mix_ref, *, n_exp):
    rows, width = mix_ref.shape
    exp_dev = out_ref.shape[0]
    upstream = g_ref[...].astype(f32)
    lanes = lax.broadcasted_iota(jnp.int32, (rows, LANES), 1)
    mix = jnp.zeros((rows, width), f32)
    back = jnp.zeros((rows, width), f32)
    tail = jnp.zeros((rows, LANES), f32)
    for j in range(exp_dev):
        pick = pick_matrix(aux_ref[:, exp_dev + j : exp_dev + j + 1], out_ref.shape[2])
        picked = dot_plain(pick, out_ref[j, 0])
        mix = mix + aux_ref[:, j : j + 1] * picked
        back = back + dot_plain(pick, rows_ref[j, 0])
        prob = jnp.sum(picked * upstream, axis=1, keepdims=True)
        high = prob.astype(bf16).astype(f32)
        expert = fsdp_ref[0] * exp_dev + j
        tail = jnp.where(lanes == expert, high, tail)
        tail = jnp.where(lanes == n_exp + expert, prob - high, tail)
    mix_ref[...] = mix.astype(bf16)
    back_ref[:, :width] = back.astype(bf16)
    back_ref[:, width:] = tail.astype(bf16)


def combine(fsdp_at, produced, rows_grad, aux, g_all, n_exp, block_len):
    exp_dev, n_groups, slots, width = produced.shape
    rows = GROUP * block_len
    total_rows = n_groups * rows
    slot_spec = pl.BlockSpec((exp_dev, 1, slots, width), lambda i, s: (0, i, 0, 0))
    row_spec = pl.BlockSpec((rows, width), lambda i, s: (i, 0))
    return pl.pallas_call(
        functools.partial(combine_kernel, n_exp=n_exp),
        grid_spec=pltpu.PrefetchScalarGridSpec(
            num_scalar_prefetch=1,
            grid=(n_groups,),
            in_specs=[
                slot_spec,
                slot_spec,
                pl.BlockSpec((rows, LANES), lambda i, s: (i, 0)),
                row_spec,
            ],
            out_specs=[pl.BlockSpec((rows, width + LANES), lambda i, s: (i, 0)), row_spec],
        ),
        out_shape=[
            jax.ShapeDtypeStruct((total_rows, width + LANES), bf16),
            jax.ShapeDtypeStruct((total_rows, width), bf16),
        ],
        compiler_params=params(1),
        cost_estimate=cost(
            4 * exp_dev * total_rows * slots * width, 4 * total_rows * width * (2 + exp_dev)
        ),
        name="combine",
    )(fsdp_at.reshape(1), produced, rows_grad, aux, g_all)


def per_device(tokens, out_grad, w_qkv, w_out, router, gains, experts, seg_ids, routes):
    block_len = seg_ids.shape[1]
    rows_dev, width = tokens.shape
    n_exp = router.shape[1]
    exp_dev = experts.shape[1]
    top_count = routes.shape[1]
    n_fsdp = lax.axis_size("fsdp")
    rep_at = lax.axis_index("rep")
    fsdp_at = lax.axis_index("fsdp")
    capacity = max(2, block_len * top_count * 5 // (4 * n_exp))
    att_scale = HEAD_DIM ** (-0.5)
    shard = w_qkv.shape[0]
    part = width // 4
    heads = part // HEAD_DIM
    group_rows = 4 * rows_dev
    n_blocks = group_rows // block_len

    e_own = experts.transpose(1, 2, 0, 3)
    e_far = far(e_own)
    e_parts = [e_own, near(e_own), e_far, near(e_far)]

    tok_ext = jnp.concatenate(
        [tokens, jnp.pad(seg_ids.reshape(rows_dev, 1), ((0, 0), (0, LANES - 1))).astype(bf16)],
        axis=1,
    )
    tok_all = rep_gather(tok_ext).reshape(group_rows, width + LANES)
    inputs_all = tok_all[:, :width].astype(f32)
    seg_all = tok_all[:, width].astype(jnp.int32).reshape(n_blocks, block_len)
    inputs = tokens.astype(f32)
    upstream = out_grad.astype(f32)

    columns = w_qkv.reshape(shard, 3, 4, part)

    def column_group(q):
        return lax.dynamic_index_in_dim(columns, rep_at ^ q, 2, keepdims=False).reshape(
            shard, 3 * part
        )

    got = far(jnp.stack([column_group(2), column_group(3)]))
    got2 = near(jnp.stack([column_group(1), got[1]]))
    w_rows = by_rep(jnp.stack([column_group(0), got2[0], got[0], got2[1]]), rep_at)
    small = jnp.concatenate(
        [router, gains.T, jnp.zeros((shard, LANES - (n_exp + 4) % LANES), bf16)], axis=1
    )
    small_cols = small.shape[1]
    small_rows = by_rep(rep_gather(small), rep_at)
    w_full = fsdp_gather(jnp.concatenate([w_rows, small_rows], axis=2), axis=1).reshape(
        width, 3 * part + small_cols
    )
    w_heads = w_full[:, : 3 * part]
    small_full = w_full[:, 3 * part :]
    full_router = small_full[:, :n_exp]
    gain_f = small_full[:, n_exp : n_exp + 4].astype(f32).T
    o_heads = fsdp_gather(w_out)
    gain_q = lax.dynamic_slice_in_dim(gain_f[1], rep_at * part, part, 0)
    gain_k = lax.dynamic_slice_in_dim(gain_f[2], rep_at * part, part, 0)

    g_ext = jnp.concatenate(
        [out_grad, jnp.pad(routes, ((0, 0), (0, LANES - top_count))).astype(bf16)], axis=1
    )
    g_all = fsdp_gather(g_ext)

    scale_one_all = rms_scale(inputs_all)
    normed_all = (inputs_all * scale_one_all * gain_f[0]).astype(bf16)
    qkv_rows = dot_plain(normed_all, w_heads)
    q_raw = qkv_rows[:, :part]
    k_raw = qkv_rows[:, part : 2 * part]
    v_raw = qkv_rows[:, 2 * part :]
    squares = jnp.stack([jnp.sum(q_raw * q_raw, axis=1), jnp.sum(k_raw * k_raw, axis=1)])
    squares = rep_total(squares.reshape(2, 4, rows_dev).transpose(1, 0, 2))
    squares = squares.transpose(1, 0, 2).reshape(2, group_rows, 1)
    q_scale = lax.rsqrt(squares[0] / width + epsilon)
    k_scale = lax.rsqrt(squares[1] / width + epsilon)
    shape4 = (n_blocks, block_len, heads, HEAD_DIM)
    q_norm = (q_raw * q_scale * gain_q).reshape(shape4)
    k_norm = (k_raw * k_scale * gain_k).reshape(shape4)
    cosine, sine = rope_tables(seg_all)
    cosine = cosine[:, :, None, :]
    sine = sine[:, :, None, :]
    queries = (q_norm * cosine + rotate_half(q_norm) * sine).astype(bf16)
    key_rot = (k_norm * cosine + rotate_half(k_norm) * sine).astype(bf16)
    values_h = v_raw.reshape(shape4).astype(bf16)
    allowed = causal_mask(seg_all)[:, None]
    scores = (
        jnp.einsum("bqhd,bkhd->bhqk", queries, key_rot, preferred_element_type=f32) * att_scale
    )
    masked = jnp.where(allowed, scores, -1e30)
    top_score = jnp.max(masked, axis=-1, keepdims=True)
    expd = jnp.exp(masked - top_score)
    totals = jnp.sum(expd, axis=-1, keepdims=True)
    probs = expd / totals
    probs_low = probs.astype(bf16)
    mixed_rows = (
        jnp.einsum("bhqk,bkhd->bqhd", probs_low, values_h, preferred_element_type=f32)
        .reshape(group_rows, part)
        .astype(bf16)
    )
    out_parts = dot_plain(mixed_rows, o_heads).reshape(4, rows_dev, width)
    hidden = inputs + rep_scatter_sum(out_parts)
    scale_two = rms_scale(hidden)
    normed2 = (hidden * scale_two * gain_f[3]).astype(bf16)

    n2_all = fsdp_gather(normed2)
    rows_in, rows_up, aux = dispatch(
        fsdp_at, n2_all, g_all, small_full, n_exp, exp_dev, capacity, block_len
    )
    slot_shape = rows_in.shape
    rows_in = rows_in.reshape(exp_dev, -1, width)
    rows_up = rows_up.reshape(exp_dev, -1, width)
    produced, rows_grad, active, bars = ffn(rows_in, rows_up, e_parts)
    back_part, mix_part = combine(
        fsdp_at,
        produced.reshape(slot_shape),
        rows_grad.reshape(slot_shape),
        aux,
        g_all,
        n_exp,
        block_len,
    )
    back_got = fsdp_scatter_sum(back_part)
    input_grad = back_got[:, :width].astype(f32)
    prob_grad = back_got[:, width : width + n_exp].astype(f32) + back_got[
        :, width + n_exp : width + 2 * n_exp
    ].astype(f32)
    mix_got = fsdp_scatter_sum(mix_part)
    layer_out = (hidden + mix_got.astype(f32)).astype(bf16)

    grad_near, grad_own = ffn_grad(rows_in, rows_up, active, bars)
    e_got = near(grad_near).astype(f32)
    e_sent = far((grad_own[1].astype(f32) + e_got[1]).astype(bf16)).astype(f32)
    expert_grad = (grad_own[0].astype(f32) + e_got[0] + e_sent).transpose(2, 0, 1, 3)

    gate_probs = jax.nn.softmax(dot_plain(normed2, full_router), axis=-1)
    logit_grad = (
        gate_probs * (prob_grad - jnp.sum(prob_grad * gate_probs, axis=-1, keepdims=True))
    ).astype(bf16)
    normed2_grad = dot_right_t(logit_grad, full_router) + input_grad
    hidden_grad = upstream + norm_back(hidden, scale_two, gain_f[3], normed2_grad)
    gain_three = jnp.sum(normed2_grad * hidden * scale_two, axis=0)
    router_part = dot_left_t(normed2, logit_grad)

    attn_grad = rep_gather(hidden_grad.astype(bf16)).reshape(group_rows, width)
    mixed_grad = dot_right_t(attn_grad, o_heads).astype(bf16)
    mixed_grad4 = mixed_grad.reshape(shape4)
    weight_grad = jnp.einsum("bqhd,bkhd->bhqk", mixed_grad4, values_h, preferred_element_type=f32)
    inner_sum = jnp.sum(probs * weight_grad, axis=-1, keepdims=True)
    score_grad = (probs * (weight_grad - inner_sum) * att_scale).astype(bf16)
    query_grad = jnp.einsum("bhqk,bkhd->bqhd", score_grad, key_rot, preferred_element_type=f32)
    key_grad = jnp.einsum("bhqk,bqhd->bkhd", score_grad, queries, preferred_element_type=f32)
    value_grad = jnp.einsum("bhqk,bqhd->bkhd", probs_low, mixed_grad4, preferred_element_type=f32)
    qn_grad = (query_grad * cosine - rotate_half(query_grad * sine)).reshape(group_rows, part)
    kn_grad = (key_grad * cosine - rotate_half(key_grad * sine)).reshape(group_rows, part)
    q_gain = qn_grad * q_raw
    k_gain = kn_grad * k_raw
    inner = jnp.stack([jnp.sum(q_gain * gain_q, axis=1), jnp.sum(k_gain * gain_k, axis=1)])
    inner = rep_total(inner.reshape(2, 4, rows_dev).transpose(1, 0, 2))
    inner = inner.transpose(1, 0, 2).reshape(2, group_rows, 1) / width
    gain_one = jnp.sum(q_gain * q_scale, axis=0)
    gain_two = jnp.sum(k_gain * k_scale, axis=0)
    q_part = q_scale * (gain_q * qn_grad) - q_raw * (q_scale * q_scale * q_scale) * inner[0]
    k_part = k_scale * (gain_k * kn_grad) - k_raw * (k_scale * k_scale * k_scale) * inner[1]
    qkv_grad = jnp.concatenate(
        [q_part, k_part, value_grad.reshape(group_rows, part)], axis=1
    ).astype(bf16)
    normed_grad = rep_scatter_sum(dot_right_t(qkv_grad, w_heads).reshape(4, rows_dev, width))
    scale_one = rms_scale(inputs)
    tokens_grad = hidden_grad + norm_back(inputs, scale_one, gain_f[0], normed_grad)
    gain_zero = jnp.sum(normed_grad * inputs * scale_one, axis=0)

    gain_rows = jnp.stack(
        [
            gain_zero,
            lax.dynamic_update_slice(jnp.zeros((width,), f32), gain_one, (rep_at * part,)),
            lax.dynamic_update_slice(jnp.zeros((width,), f32), gain_two, (rep_at * part,)),
            gain_three,
        ]
    )
    small_grad = jnp.concatenate(
        [router_part, gain_rows.T, jnp.zeros((width, small_cols - n_exp - 4), f32)], axis=1
    )
    w_grad = jnp.concatenate([dot_left_t(normed_all, qkv_grad), small_grad], axis=1)
    w_grad = w_grad.astype(bf16).reshape(4, n_fsdp, shard, 3 * part + small_cols)
    w_got = fsdp_scatter_sum(
        w_grad.transpose(1, 0, 2, 3).reshape(n_fsdp * 4 * shard, 3 * part + small_cols)
    ).reshape(4, shard, 3 * part + small_cols)
    rel = by_rep(w_got, rep_at)
    pair_far = far(jnp.stack([rel[2], rel[3]]))
    pair_near = near(jnp.stack([rel[1], pair_far[1]]))
    col_groups = by_rep(
        jnp.stack([rel[0], pair_near[0], pair_far[0], pair_near[1]])[:, :, : 3 * part], rep_at
    )
    grad_qkv = (
        col_groups.reshape(4, shard, 3, part)
        .transpose(1, 2, 0, 3)
        .reshape(shard, 12 * part)
        .astype(f32)
    )
    small_got = (
        rel[0][:, 3 * part :].astype(f32)
        + pair_near[0][:, 3 * part :].astype(f32)
        + pair_far[0][:, 3 * part :].astype(f32)
        + pair_near[1][:, 3 * part :].astype(f32)
    )
    grad_wout = fsdp_scatter_sum(dot_left_t(mixed_rows, attn_grad).astype(bf16)).astype(f32)
    return (
        layer_out,
        tokens_grad,
        grad_qkv,
        grad_wout,
        small_got[:, :n_exp],
        small_got[:, n_exp : n_exp + 4].T,
        expert_grad,
    )


def solution(mesh):
    in_specs = (
        P(("rep", "fsdp"), None),
        P(("rep", "fsdp"), None),
        P(("rep", "fsdp"), None),
        P(("rep", "fsdp"), None),
        P(("rep", "fsdp"), None),
        P(None, ("rep", "fsdp")),
        P("rep", "fsdp", None, None),
        P(("rep", "fsdp"), None),
        P(("rep", "fsdp"), None),
    )
    out_specs = (
        P(("rep", "fsdp"), None),
        P(("rep", "fsdp"), None),
        P(("rep", "fsdp"), None),
        P(("rep", "fsdp"), None),
        P(("rep", "fsdp"), None),
        P(None, ("rep", "fsdp")),
        P("rep", "fsdp", None, None),
    )
    return jax.shard_map(
        per_device, mesh=mesh, in_specs=in_specs, out_specs=out_specs, check_vma=False
    )
```

```python
import functools

import jax
import jax.numpy as jnp
from jax import lax
from jax.experimental import pallas as pl
from jax.experimental.pallas import tpu as pltpu
from jax.sharding import PartitionSpec as P


HEAD_DIM = 128
LANES = 128
GROUP = 4
TOP_LANES = 8

epsilon = 1e-05
rope_base = 10000.0
bf16 = jnp.bfloat16
f32 = jnp.float32


def dot_plain(left_side, right_side):
    return jnp.dot(left_side, right_side, preferred_element_type=f32)


def dot_left_t(left_side, right_side):
    return lax.dot_general(
        left_side, right_side, (((0,), (0,)), ((), ())), preferred_element_type=f32
    )


def dot_right_t(left_side, right_side):
    return lax.dot_general(
        left_side, right_side, (((1,), (1,)), ((), ())), preferred_element_type=f32
    )


def rms_scale(values):
    return lax.rsqrt(jnp.mean(values * values, axis=-1, keepdims=True) + epsilon)


def norm_back(values, row_scale, gain_row, upstream):
    weighted = gain_row * upstream
    inner_sum = jnp.mean(weighted * values, axis=-1, keepdims=True)
    return row_scale * weighted - values * (row_scale * row_scale * row_scale) * inner_sum


def hop(value, q):
    return lax.ppermute(value, "rep", [(i, i ^ q) for i in range(4)])


def near(value):
    return hop(value, 1)


def far(value):
    return hop(value, 2)


def rep_gather(value):
    across = far(value)
    beside = near(value)
    corner = near(across)
    return [value, beside, across, corner]


def rep_sum(near_parts, home_parts):
    got = near(near_parts)
    sent = far((home_parts[1].astype(f32) + got[1].astype(f32)).astype(bf16))
    return home_parts, got, sent


def along(value, move, first, last):
    return lax.ppermute(
        value,
        "fsdp",
        [(2 * i + j, 2 * (i + move) + j) for i in range(first, last + 1) for j in range(2)],
    )


def across(value, first=0, last=3):
    return lax.ppermute(
        value, "fsdp", [(2 * i + j, 2 * i + 1 - j) for i in range(first, last + 1) for j in range(2)]
    )


def fsdp_gather(value, axis=0):
    if lax.axis_size("fsdp") != 8:
        return lax.all_gather(value, "fsdp", axis=axis, tiled=False), ()
    at = lax.axis_index("fsdp")
    line, side = at // 2, at % 2
    up, down = [value], [value]
    side_up, side_down = [across(value)], [None]
    for s in range(1, 4):
        up.append(along(up[-1], 1, s - 1, 2))
        down.append(along(down[-1], -1, 1, 4 - s))
        side_up.append(across(up[s], s, 3))
        side_down.append(across(down[s], 0, 3 - s))
    shape = value.shape[:axis] + (8,) + value.shape[axis:]
    out = jnp.zeros(shape, value.dtype)

    def put(out, chunk, index):
        return lax.dynamic_update_slice_in_dim(out, jnp.expand_dims(chunk, axis), index, axis)

    out = put(put(out, value, at), side_up[0], at ^ 1)
    for s in range(1, 4):
        pair = 2 * ((line - s) % 4)
        below = line >= s
        out = put(out, jnp.where(below, up[s], down[4 - s]), pair + side)
        out = put(out, jnp.where(below, side_up[s], side_down[4 - s]), pair + 1 - side)
    return out, (up[3], down[3])


def fsdp_scatter_sum(value, axis=0, hold=()):
    n_fsdp = lax.axis_size("fsdp")
    if n_fsdp != 8:
        moved = jnp.moveaxis(value, axis, 0)
        return lax.psum_scatter(moved, "fsdp", scatter_dimension=0, tiled=False).astype(f32)
    at = lax.axis_index("fsdp")
    line, side = at // 2, at % 2

    pairs = [2 * ((line + m) % 4) for m in range(4)]
    sent = lax.optimization_barrier(
        [
            lax.dynamic_index_in_dim(value, pair + 1 - side, axis, keepdims=False)
            for pair in pairs
        ]
    )
    got = {}
    for m in (3, 1, 2, 0):
        got[m] = across(sent[m])

    if hold:
        got[3] = after(got[3], *hold)
        got[1] = after(got[1], *hold)

    def total(m, *more, dtype=bf16):
        return add_entry(value, pairs[m] + side, axis, (got[m],) + more, dtype)

    up = along(total(3), 1, 0, 0)
    down = along(total(1), -1, 3, 3)
    up = along(total(2, up), 1, 0, 1)
    down = along(total(2, down), -1, 2, 3)
    up = along(total(1, up), 1, 0, 2)
    down = along(total(3, down), -1, 1, 3)
    return total(0, up, down, dtype=f32)


def after(value, *others):
    return lax.optimization_barrier((value, *others))[0]


def cost(flops, bytes_accessed):
    return pl.CostEstimate(flops=flops, bytes_accessed=bytes_accessed, transcendentals=0)


def params(semantics):
    return pltpu.CompilerParams(
        dimension_semantics=("arbitrary",) * semantics, vmem_limit_bytes=60 << 20
    )


def add_kernel(at_ref, *refs):
    total = refs[0][...].astype(f32)
    for ref in refs[1:-1]:
        total = total + ref[...].astype(f32).reshape(total.shape)
    refs[-1][...] = total.reshape(refs[-1].shape).astype(refs[-1].dtype)


def add_entry(value, index, axis, others, dtype):
    shape = others[0].shape
    whole = tuple(0 for _ in shape)
    if axis:
        own = pl.BlockSpec((shape[0], 1) + shape[1:], lambda i, at: (0, at[0], 0, 0))
    else:
        own = pl.BlockSpec((1,) + shape, lambda i, at: (at[0],) + whole)
    spec = pl.BlockSpec(shape, lambda i, at: whole)
    return pl.pallas_call(
        add_kernel,
        grid_spec=pltpu.PrefetchScalarGridSpec(
            num_scalar_prefetch=1,
            grid=(1,),
            in_specs=[own] + [spec] * len(others),
            out_specs=spec,
        ),
        out_shape=jax.ShapeDtypeStruct(shape, dtype),
        compiler_params=pltpu.CompilerParams(vmem_limit_bytes=32 << 20),
        name="add_entry",
    )(index.reshape(1).astype(jnp.int32), value, *others)


def pack_kernel(rep_ref, w_ref, small_ref, *out_refs):
    part = w_ref.shape[1] // 12
    for q, out_ref in enumerate(out_refs):
        for c in range(3):
            start = pl.multiple_of((4 * c + (rep_ref[0] ^ q)) * part, part)
            out_ref[:, c * part : (c + 1) * part] = w_ref[:, pl.ds(start, part)]
        out_ref[:, 3 * part :] = small_ref[...]


def pack(rep_at, w_qkv, small):
    shard = w_qkv.shape[0]
    piece = jax.ShapeDtypeStruct((shard, w_qkv.shape[1] // 4 + small.shape[1]), bf16)
    return pl.pallas_call(
        pack_kernel,
        in_specs=[
            pl.BlockSpec(memory_space=pltpu.SMEM),
            pl.BlockSpec(memory_space=pltpu.VMEM),
            pl.BlockSpec(memory_space=pltpu.VMEM),
        ],
        out_specs=[pl.BlockSpec(memory_space=pltpu.VMEM)] * 4,
        out_shape=[piece] * 4,
        name="pack",
    )(rep_at.reshape(1), w_qkv, small)


def chunk_kernel(rep_ref, p0, p1, p2, p3, o_ref, out_ref):
    part = o_ref.shape[1] // 4
    for q, piece in enumerate((p0, p1, p2, p3)):
        row = rep_ref[0] ^ q
        out_ref[row, :, : 3 * part] = piece[:, : 3 * part]
        out_ref[row, :, 4 * part :] = piece[:, 3 * part :]
        out_ref[q, :, 3 * part : 4 * part] = o_ref[:, q * part : (q + 1) * part]


def chunk_of(rep_at, pieces, w_out):
    shard, width = w_out.shape
    lanes = pieces[0].shape[1] + width // 4
    return pl.pallas_call(
        chunk_kernel,
        in_specs=[pl.BlockSpec(memory_space=pltpu.SMEM)]
        + [pl.BlockSpec(memory_space=pltpu.VMEM)] * 5,
        out_specs=pl.BlockSpec(memory_space=pltpu.VMEM),
        out_shape=jax.ShapeDtypeStruct((4, shard, lanes), bf16),
        name="chunk",
    )(rep_at.reshape(1), *pieces, w_out)


def pick_matrix(slot_column, slot_count):
    ids = lax.broadcasted_iota(jnp.int32, (slot_column.shape[0], slot_count), 1).astype(f32)
    return jnp.where(slot_column == ids, 1.0, 0.0).astype(bf16)


def dispatch_kernel(
    fsdp_ref, n2_ref, ext_ref, router_ref, x_ref, up_ref, aux_ref, *, n_exp, capacity, block_len
):
    rows, width = n2_ref.shape
    exp_dev = x_ref.shape[0]
    first = fsdp_ref[0] * exp_dev
    normed2 = n2_ref[...]
    lanes = lax.broadcasted_iota(jnp.int32, (rows, LANES), 1)
    logits = jnp.where(lanes < n_exp, dot_plain(normed2, router_ref[...]), -1e30)
    expd = jnp.exp(logits - jnp.max(logits, axis=1, keepdims=True))
    probs = expd / jnp.sum(expd, axis=1, keepdims=True)
    tail = ext_ref[:, width:].astype(f32)
    upstream = ext_ref[:, :width].astype(f32)
    at_row = lax.broadcasted_iota(jnp.int32, (rows, rows), 0)
    at_col = lax.broadcasted_iota(jnp.int32, (rows, rows), 1)
    earlier = jnp.where(
        (at_row // block_len == at_col // block_len) & (at_col < at_row), 1.0, 0.0
    ).astype(bf16)
    named = [
        jnp.max(
            jnp.where((tail == (first + j).astype(f32)) & (lanes < TOP_LANES), 1.0, 0.0),
            axis=1,
            keepdims=True,
        )
        for j in range(exp_dev)
    ]
    hit_lanes = jnp.zeros((rows, LANES), f32)
    for j in range(exp_dev):
        hit_lanes = jnp.where(lanes == j, named[j], hit_lanes)
    prior = dot_plain(earlier, hit_lanes.astype(bf16))
    base = (lax.broadcasted_iota(jnp.int32, (rows, 1), 0) // block_len * capacity).astype(f32)
    aux = jnp.zeros((rows, LANES), f32)
    for j in range(exp_dev):
        chosen = jnp.sum(jnp.where(lanes == first + j, probs, 0.0), axis=1, keepdims=True)
        slot = jnp.where(named[j] > 0.5, prior[:, j : j + 1] + base, -1.0)
        pick = pick_matrix(slot, x_ref.shape[2])
        x_ref[j, 0] = dot_left_t(pick, normed2).astype(bf16)
        up_ref[j, 0] = dot_left_t(pick, (chosen * upstream).astype(bf16)).astype(bf16)
        aux = jnp.where(lanes == j, chosen, aux)
        aux = jnp.where(lanes == exp_dev + j, slot, aux)
    aux_ref[...] = aux


def dispatch(fsdp_at, n2_all, g_all, w_full, n_exp, exp_dev, capacity, block_len):
    total_rows, width = n2_all.shape
    rows = GROUP * block_len
    n_groups = total_rows // rows
    slots = GROUP * capacity
    small_at = w_full.shape[1] // LANES - 1
    slot_spec = pl.BlockSpec((exp_dev, 1, slots, width), lambda i, s: (0, i, 0, 0))
    slot_shape = jax.ShapeDtypeStruct((exp_dev, n_groups, slots, width), bf16)
    return pl.pallas_call(
        functools.partial(
            dispatch_kernel, n_exp=n_exp, capacity=capacity, block_len=block_len
        ),
        grid_spec=pltpu.PrefetchScalarGridSpec(
            num_scalar_prefetch=1,
            grid=(n_groups,),
            in_specs=[
                pl.BlockSpec((rows, width), lambda i, s: (i, 0)),
                pl.BlockSpec((rows, g_all.shape[1]), lambda i, s: (i, 0)),
                pl.BlockSpec((width, LANES), lambda i, s: (0, small_at)),
            ],
            out_specs=[slot_spec, slot_spec, pl.BlockSpec((rows, LANES), lambda i, s: (i, 0))],
        ),
        out_shape=[slot_shape, slot_shape, jax.ShapeDtypeStruct((total_rows, LANES), f32)],
        compiler_params=params(1),
        cost_estimate=cost(
            4 * exp_dev * total_rows * slots * width, 4 * total_rows * width * (2 + exp_dev)
        ),
        name="dispatch",
    )(fsdp_at.reshape(1), n2_all, g_all, w_full)


def ffn_kernel(
    x_ref, up_ref, e0, e1, p2, d2, p3, d3, out_ref, back_ref, act_ref, bar_ref,
    weights, out_acc, back_acc, sems,
):
    j = pl.program_id(0)
    t = pl.program_id(1)
    step = j * 4 + t

    def fetch(at_j, at_t, slot, go):
        sources = (
            ((e0, 0, 2), (e0, 2, 1)),
            ((e1, 0, 2), (e1, 2, 1)),
            ((p2, 0, 2), (d2, 0, 1)),
            ((p3, 0, 2), (d3, 0, 1)),
        )
        for q, pieces in enumerate(sources):

            @pl.when(at_t == q)
            def _():
                for i, (ref, first, count) in enumerate(pieces):
                    copy = pltpu.make_async_copy(
                        ref.at[at_j, pl.ds(first, count)],
                        weights.at[slot, pl.ds(2 * i, count)],
                        sems.at[slot, i],
                    )
                    copy.start() if go else copy.wait()

    @pl.when(step == 0)
    def _():
        fetch(j, t, 0, True)

    @pl.when(step + 1 < 4 * pl.num_programs(0))
    def _():
        following = step + 1
        fetch(following // 4, following % 4, following % 2, True)

    fetch(j, t, step % 2, False)
    slot = step % 2
    hidden = weights.shape[2]
    width = x_ref.shape[2]
    pair = weights[slot, 0:2].reshape(2 * hidden, width)
    down = weights[slot, 2]
    pre = dot_right_t(x_ref[0], pair)
    gate_pre = pre[:, :hidden]
    up_pre = pre[:, hidden:]
    sig = jax.nn.sigmoid(gate_pre)
    active = (gate_pre * sig * up_pre).astype(bf16)
    act_ref[0, 0] = active
    grad = dot_right_t(up_ref[0], down)
    up_bar = grad * (gate_pre * sig)
    gate_bar = grad * up_pre * sig * (1.0 + gate_pre * (1.0 - sig))
    bar_ref[0, 0, :, :hidden] = gate_bar.astype(bf16)
    bar_ref[0, 0, :, hidden:] = up_bar.astype(bf16)

    @pl.when(t == 0)
    def _():
        out_acc[...] = dot_plain(active, down)
        back_acc[...] = dot_plain(bar_ref[0, 0], pair)

    @pl.when(t > 0)
    def _():
        out_acc[...] += dot_plain(active, down)
        back_acc[...] += dot_plain(bar_ref[0, 0], pair)

    @pl.when(t == 3)
    def _():
        out_ref[0] = out_acc[...].astype(bf16)
        back_ref[0] = back_acc[...].astype(bf16)


def ffn(rows_in, rows_up, e_parts):
    exp_dev, rows, width = rows_in.shape
    hidden = e_parts[0].shape[2]
    row_spec = pl.BlockSpec((1, rows, width), lambda j, t: (j, 0, 0))
    row_shape = jax.ShapeDtypeStruct((exp_dev, rows, width), bf16)
    return pl.pallas_call(
        ffn_kernel,
        grid=(exp_dev, 4),
        in_specs=[row_spec, row_spec] + [pl.BlockSpec(memory_space=pl.ANY)] * 6,
        out_specs=[
            row_spec,
            row_spec,
            pl.BlockSpec((1, 1, rows, hidden), lambda j, t: (j, t, 0, 0)),
            pl.BlockSpec((1, 1, rows, 2 * hidden), lambda j, t: (j, t, 0, 0)),
        ],
        out_shape=[
            row_shape,
            row_shape,
            jax.ShapeDtypeStruct((exp_dev, 4, rows, hidden), bf16),
            jax.ShapeDtypeStruct((exp_dev, 4, rows, 2 * hidden), bf16),
        ],
        scratch_shapes=[
            pltpu.VMEM((2, 3, hidden, width), bf16),
            pltpu.VMEM((rows, width), f32),
            pltpu.VMEM((rows, width), f32),
            pltpu.SemaphoreType.DMA((2, 2)),
        ],
        compiler_params=params(2),
        cost_estimate=cost(
            2 * exp_dev * rows * width * hidden * 4 * 6,
            2 * exp_dev * (4 * rows * width + 12 * hidden * (width + rows)),
        ),
        name="ffn",
    )(rows_in, rows_up, *e_parts)


def part_of(t):
    return jnp.where(t < 2, 2 * t + 1, 2 * t - 4)


def near_slot(t):
    return jnp.minimum(t, 1)


def home_slot(t):
    return jnp.maximum(t - 2, 0)


def ffn_grad_kernel(
    x_ref, up_ref, act_ref, bar_ref, near_pair, near_down, home_pair, home_down
):
    t = pl.program_id(1)
    hidden = act_ref.shape[3]

    def write(pair_ref, down_ref):
        pair = dot_left_t(bar_ref[0, 0], x_ref[0]).astype(bf16)
        pair_ref[0, 0, 0] = pair[:hidden]
        pair_ref[0, 0, 1] = pair[hidden:]
        down_ref[0, 0] = dot_left_t(act_ref[0, 0], up_ref[0]).astype(bf16)

    @pl.when(t < 2)
    def _():
        write(near_pair, near_down)

    @pl.when(t >= 2)
    def _():
        write(home_pair, home_down)


def ffn_grad(rows_in, rows_up, active, bars):
    exp_dev, rows, width = rows_in.shape
    hidden = active.shape[3]
    row_spec = pl.BlockSpec((1, rows, width), lambda j, t: (j, 0, 0))
    pair_shape = jax.ShapeDtypeStruct((2, exp_dev, 2, hidden, width), bf16)
    down_shape = jax.ShapeDtypeStruct((2, exp_dev, hidden, width), bf16)
    pair_block = (1, 1, 2, hidden, width)
    down_block = (1, 1, hidden, width)
    return pl.pallas_call(
        ffn_grad_kernel,
        grid=(exp_dev, 4),
        in_specs=[
            row_spec,
            row_spec,
            pl.BlockSpec((1, 1, rows, hidden), lambda j, t: (j, part_of(t), 0, 0)),
            pl.BlockSpec((1, 1, rows, 2 * hidden), lambda j, t: (j, part_of(t), 0, 0)),
        ],
        out_specs=[
            pl.BlockSpec(pair_block, lambda j, t: (near_slot(t), j, 0, 0, 0)),
            pl.BlockSpec(down_block, lambda j, t: (near_slot(t), j, 0, 0)),
            pl.BlockSpec(pair_block, lambda j, t: (home_slot(t), j, 0, 0, 0)),
            pl.BlockSpec(down_block, lambda j, t: (home_slot(t), j, 0, 0)),
        ],
        out_shape=[pair_shape, down_shape, pair_shape, down_shape],
        compiler_params=params(2),
        cost_estimate=cost(
            2 * exp_dev * rows * width * hidden * 4 * 3,
            2 * exp_dev * (2 * rows * width + 12 * hidden * (width + rows)),
        ),
        name="ffn_grad",
    )(rows_in, rows_up, active, bars)


def combine_kernel(fsdp_ref, out_ref, rows_ref, aux_ref, g_ref, back_ref, mix_ref, *, n_exp):
    rows, width = mix_ref.shape
    exp_dev = out_ref.shape[0]
    upstream = g_ref[...].astype(f32)
    lanes = lax.broadcasted_iota(jnp.int32, (rows, LANES), 1)
    mix = jnp.zeros((rows, width), f32)
    back = jnp.zeros((rows, width), f32)
    tail = jnp.zeros((rows, LANES), f32)
    for j in range(exp_dev):
        pick = pick_matrix(aux_ref[:, exp_dev + j : exp_dev + j + 1], out_ref.shape[2])
        picked = dot_plain(pick, out_ref[j, 0])
        mix = mix + aux_ref[:, j : j + 1] * picked
        back = back + dot_plain(pick, rows_ref[j, 0])
        prob = jnp.sum(picked * upstream, axis=1, keepdims=True)
        high = prob.astype(bf16).astype(f32)
        expert = fsdp_ref[0] * exp_dev + j
        tail = jnp.where(lanes == expert, high, tail)
        tail = jnp.where(lanes == n_exp + expert, prob - high, tail)
    mix_ref[...] = mix.astype(bf16)
    back_ref[:, :width] = back.astype(bf16)
    back_ref[:, width:] = tail.astype(bf16)


def combine(fsdp_at, produced, rows_grad, aux, g_all, n_exp, block_len):
    exp_dev, n_groups, slots, width = produced.shape
    rows = GROUP * block_len
    total_rows = n_groups * rows
    slot_spec = pl.BlockSpec((exp_dev, 1, slots, width), lambda i, s: (0, i, 0, 0))
    row_spec = pl.BlockSpec((rows, width), lambda i, s: (i, 0))
    return pl.pallas_call(
        functools.partial(combine_kernel, n_exp=n_exp),
        grid_spec=pltpu.PrefetchScalarGridSpec(
            num_scalar_prefetch=1,
            grid=(n_groups,),
            in_specs=[
                slot_spec,
                slot_spec,
                pl.BlockSpec((rows, LANES), lambda i, s: (i, 0)),
                row_spec,
            ],
            out_specs=[pl.BlockSpec((rows, width + LANES), lambda i, s: (i, 0)), row_spec],
        ),
        out_shape=[
            jax.ShapeDtypeStruct((total_rows, width + LANES), bf16),
            jax.ShapeDtypeStruct((total_rows, width), bf16),
        ],
        compiler_params=params(1),
        cost_estimate=cost(
            4 * exp_dev * total_rows * slots * width, 4 * total_rows * width * (2 + exp_dev)
        ),
        name="combine",
    )(fsdp_at.reshape(1), produced, rows_grad, aux, g_all)


def full_spec(shape):
    return pl.BlockSpec(shape, lambda *_: tuple(0 for _ in shape))


def to_columns(rows):
    count = rows.shape[1]
    return jnp.concatenate([rows, jnp.zeros((LANES - rows.shape[0], count), f32)], axis=0).T


def qkv_kernel(t0, t1, t2, t3, gains_ref, w_ref, normed_ref, out_ref, sums_ref, squares):
    c = pl.program_id(0)
    width = normed_ref.shape[1]
    rows = t0.shape[0]

    @pl.when(c == 0)
    def _():
        for q, ref in enumerate((t0, t1, t2, t3)):
            values = ref[:, :width].astype(f32)
            normed_ref[q * rows : (q + 1) * rows] = (
                values * rms_scale(values) * gains_ref[0:1]
            ).astype(bf16)

    result = dot_plain(normed_ref[...], w_ref[...])
    out_ref[...] = result
    lanes = lax.broadcasted_iota(jnp.int32, squares.shape, 1)
    total = jnp.sum(result * result, axis=1, keepdims=True)

    @pl.when(c == 0)
    def _():
        squares[...] = jnp.where(lanes == 0, total, 0.0)

    @pl.when(c == 1)
    def _():
        squares[...] = jnp.where(lanes == 1, total, squares[...])

    @pl.when(c == 2)
    def _():
        sums_ref[...] = squares[...].T[:8]


def qkv_rows(tok_parts, gain_f, w_full):
    rows, ext = tok_parts[0].shape
    width = gain_f.shape[1]
    part = width // 4
    return pl.pallas_call(
        qkv_kernel,
        grid=(3,),
        in_specs=[full_spec((rows, ext))] * 4
        + [full_spec((4, width)), pl.BlockSpec((width, part), lambda c: (0, c))],
        out_specs=[
            full_spec((4 * rows, width)),
            pl.BlockSpec((4 * rows, part), lambda c: (0, c)),
            full_spec((8, 4 * rows)),
        ],
        out_shape=[
            jax.ShapeDtypeStruct((4 * rows, width), bf16),
            jax.ShapeDtypeStruct((4 * rows, 3 * part), f32),
            jax.ShapeDtypeStruct((8, 4 * rows), f32),
        ],
        scratch_shapes=[pltpu.VMEM((4 * rows, LANES), f32)],
        compiler_params=params(1),
        cost_estimate=cost(24 * rows * width * part, 2 * (3 * width * part + 20 * rows * part)),
        name="qkv_rows",
    )(*tok_parts, gain_f, w_full)


def scales_of(sum_refs, width):
    total = sum_refs[0][...]
    for ref in sum_refs[1:]:
        total = total + ref[...]
    columns = to_columns(total)
    return (
        lax.rsqrt(columns[:, 0:1] / width + epsilon),
        lax.rsqrt(columns[:, 1:2] / width + epsilon),
    )


def turned(values, cosine, sine):
    return values * cosine + pltpu.roll(values, HEAD_DIM // 2, 1) * sine


def head_probs(query, key, mask):
    scores = dot_right_t(query, key) * (HEAD_DIM ** (-0.5))
    masked = jnp.where(mask > 0.5, scores, -1e30)
    expd = jnp.exp(masked - jnp.max(masked, axis=1, keepdims=True))
    return expd / jnp.sum(expd, axis=1, keepdims=True)


def attn_kernel(
    rep_ref, qkv_ref, s0, s1, s2, s3, gains_ref, cos_ref, sin_ref, mask_ref, o_ref,
    mixed_ref, near_ref, home_ref,
):
    t = pl.program_id(0)
    part = mixed_ref.shape[1]
    q_scale, k_scale = scales_of((s0, s1, s2, s3), 4 * part)
    for h in range(part // HEAD_DIM):
        at = slice(h * HEAD_DIM, (h + 1) * HEAD_DIM)
        key_at = slice(part + h * HEAD_DIM, part + (h + 1) * HEAD_DIM)
        value_at = slice(2 * part + h * HEAD_DIM, 2 * part + (h + 1) * HEAD_DIM)
        q_norm = qkv_ref[:, at] * q_scale * gains_ref[1:2, at]
        k_norm = qkv_ref[:, key_at] * k_scale * gains_ref[2:3, at]
        query = turned(q_norm, cos_ref[...], sin_ref[...]).astype(bf16)
        key = turned(k_norm, cos_ref[...], sin_ref[...]).astype(bf16)
        probs = head_probs(query, key, mask_ref[...])
        mixed_ref[:, at] = dot_plain(
            probs.astype(bf16), qkv_ref[:, value_at].astype(bf16)
        ).astype(bf16)
    mixed = mixed_ref[...]
    for c in range(4):
        at = slice(c * part, (c + 1) * part)
        block = dot_plain(mixed, o_ref[at, :])

        @pl.when(t < 2)
        def _():
            near_ref[0, :, at] = block.astype(bf16)

        @pl.when(t >= 2)
        def _():
            home_ref[0, :, at] = block


def sum_specs(rows):
    return [
        pl.BlockSpec((8, rows), functools.partial(lambda q, t, s: (0, part_of(t) ^ q), q))
        for q in range(4)
    ]


def attn(rep_at, qkv, sums, gain_f, tables, w_full):
    group_rows = qkv.shape[0]
    rows = group_rows // 4
    width = gain_f.shape[1]
    part = width // 4
    table_spec = pl.BlockSpec((rows, LANES), lambda t, s: (part_of(t), 0))
    return pl.pallas_call(
        attn_kernel,
        grid_spec=pltpu.PrefetchScalarGridSpec(
            num_scalar_prefetch=1,
            grid=(4,),
            in_specs=[pl.BlockSpec((rows, 3 * part), lambda t, s: (part_of(t), 0))]
            + sum_specs(rows)
            + [pl.BlockSpec((4, part), lambda t, s: (0, s[0]))]
            + [table_spec] * 3
            + [pl.BlockSpec((width, part), lambda t, s: (0, 3))],
            out_specs=[
                pl.BlockSpec((rows, part), lambda t, s: (part_of(t), 0)),
                pl.BlockSpec((1, rows, width), lambda t, s: (near_slot(t), 0, 0)),
                pl.BlockSpec((1, rows, width), lambda t, s: (home_slot(t), 0, 0)),
            ],
        ),
        out_shape=[
            jax.ShapeDtypeStruct((group_rows, part), bf16),
            jax.ShapeDtypeStruct((2, rows, width), bf16),
            jax.ShapeDtypeStruct((2, rows, width), f32),
        ],
        compiler_params=params(1),
        cost_estimate=cost(3 * group_rows * part * width, 20 * group_rows * part),
        name="attn",
    )(rep_at.reshape(1), qkv, *sums, gain_f, *tables, w_full)


def middle_kernel(tok_ref, home_ref, got_ref, sent_ref, gains_ref, hidden_ref, normed_ref):
    hidden = (
        tok_ref[...].astype(f32)
        + home_ref[0]
        + got_ref[0].astype(f32)
        + sent_ref[...].astype(f32)
    )
    hidden_ref[...] = hidden
    normed_ref[...] = (hidden * rms_scale(hidden) * gains_ref[3:4]).astype(bf16)


def middle(tokens, terms, gain_f):
    rows, width = tokens.shape
    home_parts, got, sent = terms
    return pl.pallas_call(
        middle_kernel,
        grid=(1,),
        in_specs=[
            full_spec((rows, width)),
            full_spec((1, rows, width)),
            full_spec((1, rows, width)),
            full_spec((rows, width)),
            full_spec((4, width)),
        ],
        out_specs=[full_spec((rows, width))] * 2,
        out_shape=[
            jax.ShapeDtypeStruct((rows, width), f32),
            jax.ShapeDtypeStruct((rows, width), bf16),
        ],
        compiler_params=params(1),
        name="middle",
    )(tokens, home_parts, got, sent, gain_f)


def middle_back_kernel(
    back_ref, hidden_ref, normed_ref, g_ref, small_ref, gains_ref,
    hidden_grad_ref, attn_grad_ref, gain_ref, router_ref, *, n_exp,
):
    rows, width = hidden_ref.shape
    small = small_ref[...]
    normed2 = normed_ref[...]
    lanes = lax.broadcasted_iota(jnp.int32, (rows, LANES), 1)
    inside = lanes < n_exp
    logits = jnp.where(inside, dot_plain(normed2, small), -1e30)
    expd = jnp.exp(logits - jnp.max(logits, axis=1, keepdims=True))
    probs = expd / jnp.sum(expd, axis=1, keepdims=True)
    tail = back_ref[:, width:]
    prob_grad = jnp.where(inside, tail + pltpu.roll(tail, LANES - n_exp, 1), 0.0)
    inner = jnp.sum(prob_grad * probs, axis=1, keepdims=True)
    logit_grad = (probs * (prob_grad - inner)).astype(bf16)
    router_ref[...] = dot_left_t(normed2, logit_grad)
    normed2_grad = dot_right_t(logit_grad, small) + back_ref[:, :width]
    hidden = hidden_ref[...]
    scale = rms_scale(hidden)
    hidden_grad = g_ref[...].astype(f32) + norm_back(
        hidden, scale, gains_ref[3:4], normed2_grad
    )
    hidden_grad_ref[...] = hidden_grad
    attn_grad_ref[...] = hidden_grad.astype(bf16)
    gain_ref[...] = jnp.broadcast_to(
        jnp.sum(normed2_grad * hidden * scale, axis=0, keepdims=True), gain_ref.shape
    )


def middle_back(back_got, hidden, normed2, out_grad, w_full, gain_f, n_exp):
    rows, width = hidden.shape
    small_at = w_full.shape[1] // LANES - 1
    return pl.pallas_call(
        functools.partial(middle_back_kernel, n_exp=n_exp),
        grid=(1,),
        in_specs=[
            full_spec(back_got.shape),
            full_spec((rows, width)),
            full_spec((rows, width)),
            full_spec((rows, width)),
            pl.BlockSpec((width, LANES), lambda i: (0, small_at)),
            full_spec((4, width)),
        ],
        out_specs=[
            full_spec((rows, width)),
            full_spec((rows, width)),
            full_spec((8, width)),
            full_spec((width, LANES)),
        ],
        out_shape=[
            jax.ShapeDtypeStruct((rows, width), f32),
            jax.ShapeDtypeStruct((rows, width), bf16),
            jax.ShapeDtypeStruct((8, width), f32),
            jax.ShapeDtypeStruct((width, LANES), f32),
        ],
        compiler_params=params(1),
        name="middle_back",
    )(back_got, hidden, normed2, out_grad, w_full, gain_f)


def attn_back_kernel(
    rep_ref, a0, a1, a2, a3, qkv_ref, s0, s1, s2, s3, gains_ref, cos_ref, sin_ref, mask_ref,
    o_ref, grads_ref, inner_ref, gain_ref, all_ref,
):
    t = pl.program_id(0)
    q = part_of(t)
    part = o_ref.shape[1]
    rows = a0.shape[0]
    for at, ref in enumerate((a0, a1, a2, a3)):

        @pl.when(q == at)
        def _():
            all_ref[...] = ref[...]

    attn_grad = all_ref[...]
    mixed_grad = dot_right_t(attn_grad[:, :part], o_ref[0:part, :])
    for c in range(1, 4):
        at = slice(c * part, (c + 1) * part)
        mixed_grad = mixed_grad + dot_right_t(attn_grad[:, at], o_ref[at, :])
    mixed_grad = mixed_grad.astype(bf16)
    q_scale, k_scale = scales_of((s0, s1, s2, s3), 4 * part)
    cosine = cos_ref[...]
    sine = sin_ref[...]
    q_inner = jnp.zeros((rows, 1), f32)
    k_inner = jnp.zeros((rows, 1), f32)
    gain_rows = []
    for h in range(part // HEAD_DIM):
        at = slice(h * HEAD_DIM, (h + 1) * HEAD_DIM)
        key_at = slice(part + h * HEAD_DIM, part + (h + 1) * HEAD_DIM)
        value_at = slice(2 * part + h * HEAD_DIM, 2 * part + (h + 1) * HEAD_DIM)
        q_raw = qkv_ref[:, at]
        k_raw = qkv_ref[:, key_at]
        query = turned(q_raw * q_scale * gains_ref[1:2, at], cosine, sine).astype(bf16)
        key = turned(k_raw * k_scale * gains_ref[2:3, at], cosine, sine).astype(bf16)
        probs = head_probs(query, key, mask_ref[...])
        mixed_h = mixed_grad[:, at]
        weight_grad = dot_right_t(mixed_h, qkv_ref[:, value_at].astype(bf16))
        inner = jnp.sum(probs * weight_grad, axis=1, keepdims=True)
        score_grad = (probs * (weight_grad - inner) * (HEAD_DIM ** (-0.5))).astype(bf16)
        query_grad = dot_plain(score_grad, key)
        key_grad = dot_left_t(score_grad, query)
        grads_ref[:, value_at] = dot_left_t(probs.astype(bf16), mixed_h)
        qn_grad = query_grad * cosine - pltpu.roll(query_grad, HEAD_DIM // 2, 1) * sine
        kn_grad = key_grad * cosine - pltpu.roll(key_grad, HEAD_DIM // 2, 1) * sine
        grads_ref[:, at] = qn_grad
        grads_ref[:, key_at] = kn_grad
        q_term = qn_grad * q_raw
        k_term = kn_grad * k_raw
        q_inner = q_inner + jnp.sum(q_term * gains_ref[1:2, at], axis=1, keepdims=True)
        k_inner = k_inner + jnp.sum(k_term * gains_ref[2:3, at], axis=1, keepdims=True)
        gain_rows.append(
            (
                jnp.sum(q_term * q_scale, axis=0, keepdims=True),
                jnp.sum(k_term * k_scale, axis=0, keepdims=True),
            )
        )
    lanes = lax.broadcasted_iota(jnp.int32, (rows, LANES), 1)
    both = jnp.where(lanes == 0, q_inner, jnp.where(lanes == 1, k_inner, 0.0))
    inner_ref[...] = both.T[:8]

    @pl.when(t == 0)
    def _():
        gain_ref[...] = jnp.zeros_like(gain_ref)

    for h, (q_row, k_row) in enumerate(gain_rows):
        at = slice(h * HEAD_DIM, (h + 1) * HEAD_DIM)
        gain_ref[0:1, at] += q_row
        gain_ref[1:2, at] += k_row


def attn_back(rep_at, attn_parts, qkv, sums, gain_f, tables, w_full):
    group_rows = qkv.shape[0]
    rows = group_rows // 4
    width = gain_f.shape[1]
    part = width // 4
    by_part = lambda t, s: (part_of(t), 0)
    return pl.pallas_call(
        attn_back_kernel,
        grid_spec=pltpu.PrefetchScalarGridSpec(
            num_scalar_prefetch=1,
            grid=(4,),
            in_specs=[full_spec((rows, width))] * 4
            + [pl.BlockSpec((rows, 3 * part), by_part)]
            + sum_specs(rows)
            + [pl.BlockSpec((4, part), lambda t, s: (0, s[0]))]
            + [pl.BlockSpec((rows, LANES), by_part)] * 3
            + [pl.BlockSpec((width, part), lambda t, s: (0, 3))],
            out_specs=[
                pl.BlockSpec((rows, 3 * part), by_part),
                pl.BlockSpec((8, rows), lambda t, s: (0, part_of(t))),
                full_spec((8, part)),
                pl.BlockSpec((rows, width), by_part),
            ],
        ),
        out_shape=[
            jax.ShapeDtypeStruct((group_rows, 3 * part), f32),
            jax.ShapeDtypeStruct((8, group_rows), f32),
            jax.ShapeDtypeStruct((8, part), f32),
            jax.ShapeDtypeStruct((group_rows, width), bf16),
        ],
        compiler_params=params(1),
        cost_estimate=cost(4 * group_rows * part * width, 40 * group_rows * part),
        name="attn_back",
    )(rep_at.reshape(1), *attn_parts, qkv, *sums, gain_f, *tables, w_full)


def heads_back_kernel(
    rep_ref, grads_ref, qkv_ref, s0, s1, s2, s3, i0, i1, i2, i3, gains_ref,
    t0, t1, t2, t3, wq_ref, wk_ref, wv_ref, out_ref, near_ref, home_ref, gain_ref, tok_ref,
):
    t = pl.program_id(0)
    q = part_of(t)
    part = wq_ref.shape[1]
    width = 4 * part
    q_scale, k_scale = scales_of((s0, s1, s2, s3), width)
    total = i0[...] + i1[...] + i2[...] + i3[...]
    inner = to_columns(total) / width
    for at, ref in enumerate((t0, t1, t2, t3)):

        @pl.when(q == at)
        def _():
            tok_ref[...] = ref[:, :width]

    for c, scale in ((0, q_scale), (1, k_scale)):
        at = slice(c * part, (c + 1) * part)
        raw = qkv_ref[:, at]
        out_ref[:, at] = (
            scale * (gains_ref[c + 1 : c + 2, :] * grads_ref[:, at])
            - raw * (scale * scale * scale) * inner[:, c : c + 1]
        ).astype(bf16)
    out_ref[:, 2 * part :] = grads_ref[:, 2 * part :].astype(bf16)
    values = tok_ref[...].astype(f32)
    normed_grad = (
        dot_right_t(out_ref[:, :part], wq_ref[...])
        + dot_right_t(out_ref[:, part : 2 * part], wk_ref[...])
        + dot_right_t(out_ref[:, 2 * part :], wv_ref[...])
    )
    gain_row = jnp.sum(normed_grad * values * rms_scale(values), axis=0, keepdims=True)

    @pl.when(t == 0)
    def _():
        gain_ref[...] = jnp.zeros_like(gain_ref)

    gain_ref[0:1, :] += gain_row

    @pl.when(t < 2)
    def _():
        near_ref[0] = normed_grad.astype(bf16)

    @pl.when(t >= 2)
    def _():
        home_ref[0] = normed_grad


def heads_back(rep_at, grads, qkv, sums, inners, gain_f, tok_parts, w_full):
    group_rows = qkv.shape[0]
    rows, ext = tok_parts[0].shape
    width = gain_f.shape[1]
    part = width // 4
    by_part = lambda t, s: (part_of(t), 0)
    return pl.pallas_call(
        heads_back_kernel,
        grid_spec=pltpu.PrefetchScalarGridSpec(
            num_scalar_prefetch=1,
            grid=(4,),
            in_specs=[pl.BlockSpec((rows, 3 * part), by_part)] * 2
            + sum_specs(rows) * 2
            + [pl.BlockSpec((4, part), lambda t, s: (0, s[0]))]
            + [full_spec((rows, ext))] * 4
            + [
                pl.BlockSpec((width, part), functools.partial(lambda c, t, s: (0, c), c))
                for c in range(3)
            ],
            out_specs=[
                pl.BlockSpec((rows, 3 * part), by_part),
                pl.BlockSpec((1, rows, width), lambda t, s: (near_slot(t), 0, 0)),
                pl.BlockSpec((1, rows, width), lambda t, s: (home_slot(t), 0, 0)),
                full_spec((8, width)),
            ],
            scratch_shapes=[pltpu.VMEM((rows, width), bf16)],
        ),
        out_shape=[
            jax.ShapeDtypeStruct((group_rows, 3 * part), bf16),
            jax.ShapeDtypeStruct((2, rows, width), bf16),
            jax.ShapeDtypeStruct((2, rows, width), f32),
            jax.ShapeDtypeStruct((8, width), f32),
        ],
        compiler_params=params(1),
        cost_estimate=cost(6 * group_rows * part * width, 40 * group_rows * part),
        name="heads_back",
    )(rep_at.reshape(1), grads, qkv, *sums, *inners, gain_f, *tok_parts, w_full, w_full, w_full)


def weight_grad_kernel(
    rep_ref, normed_ref, qkv_grad_ref, mixed_ref, attn_ref, router_ref, zero_ref, mid_ref,
    three_ref, out_ref, *, n_exp,
):
    row = pl.program_id(0)
    part = mixed_ref.shape[1]
    lead = out_ref.shape[1:3]
    heads = dot_left_t(normed_ref[...], qkv_grad_ref[...]).astype(bf16)
    out_ref[0, :, :, : 3 * part] = heads.reshape(lead + (3 * part,))
    outer = dot_left_t(mixed_ref[...], attn_ref[...]).astype(bf16)
    out_ref[0, :, :, 3 * part : 4 * part] = outer.reshape(lead + (part,))
    here = jnp.where(rep_ref[0] == row, 1.0, 0.0)
    at_row = lax.broadcasted_iota(jnp.int32, (LANES, part), 0)
    gains = jnp.where(at_row == n_exp, zero_ref[0:1], 0.0)
    gains = jnp.where(at_row == n_exp + 1, here * mid_ref[0:1], gains)
    gains = jnp.where(at_row == n_exp + 2, here * mid_ref[1:2], gains)
    gains = jnp.where(at_row == n_exp + 3, three_ref[0:1], gains)
    small = (router_ref[...] + gains.T).astype(bf16)
    out_ref[0, :, :, 4 * part :] = small.reshape(lead + (LANES,))


def weight_grad(rep_at, normed, qkv_grad, mixed, attn_all, router, zero, mid, three, n_exp, lead):
    group_rows, width = normed.shape
    part = width // 4
    block = (1,) + lead + (4 * part + LANES,)
    by_row = lambda i, s: (0, i)
    return pl.pallas_call(
        functools.partial(weight_grad_kernel, n_exp=n_exp),
        grid_spec=pltpu.PrefetchScalarGridSpec(
            num_scalar_prefetch=1,
            grid=(4,),
            in_specs=[
                pl.BlockSpec((group_rows, part), by_row),
                full_spec((group_rows, 3 * part)),
                full_spec((group_rows, part)),
                pl.BlockSpec((group_rows, part), by_row),
                pl.BlockSpec((part, LANES), lambda i, s: (i, 0)),
                pl.BlockSpec((8, part), by_row),
                full_spec((8, part)),
                pl.BlockSpec((8, part), by_row),
            ],
            out_specs=pl.BlockSpec(block, lambda i, s: (i, 0, 0, 0)),
        ),
        out_shape=jax.ShapeDtypeStruct((4,) + block[1:], bf16),
        compiler_params=params(1),
        cost_estimate=cost(8 * group_rows * part * width, 20 * width * part),
        name="weight_grad",
    )(rep_at.reshape(1), normed, qkv_grad, mixed, attn_all, router, zero, mid, three)


def unpack_kernel(rep_ref, got_ref, o_ref, *piece_refs):
    part = o_ref.shape[1] // 4
    for q, piece in enumerate(piece_refs):
        row = rep_ref[0] ^ q
        o_ref[:, q * part : (q + 1) * part] = got_ref[q, :, 3 * part : 4 * part]
        piece[:, : 3 * part] = got_ref[row, :, : 3 * part].astype(bf16)
        piece[:, 3 * part :] = got_ref[row, :, 4 * part :].astype(bf16)


def unpack(rep_at, got):
    shard, lanes = got.shape[1:]
    part = (lanes - LANES) // 4
    piece = jax.ShapeDtypeStruct((shard, 3 * part + LANES), bf16)
    vmem = pl.BlockSpec(memory_space=pltpu.VMEM)
    return pl.pallas_call(
        unpack_kernel,
        in_specs=[pl.BlockSpec(memory_space=pltpu.SMEM), vmem],
        out_specs=[vmem] * 5,
        out_shape=[jax.ShapeDtypeStruct((shard, 4 * part), f32)] + [piece] * 4,
        name="unpack",
    )(rep_at.reshape(1), got)


def finish_kernel(rep_ref, p0, p1, p2, p3, w_ref, router_ref, gains_ref):
    part = w_ref.shape[1] // 12
    shard, n_exp = router_ref.shape
    small = jnp.zeros((shard, LANES), f32)
    for q, piece in enumerate((p0, p1, p2, p3)):
        for c in range(3):
            start = pl.multiple_of((4 * c + (rep_ref[0] ^ q)) * part, part)
            w_ref[:, pl.ds(start, part)] = piece[:, c * part : (c + 1) * part].astype(f32)
        small = small + piece[:, 3 * part :].astype(f32)
    router_ref[...] = small[:, :n_exp]
    square = jnp.concatenate([small, jnp.zeros((LANES - shard, LANES), f32)], axis=0).T
    gains_ref[...] = square[n_exp : n_exp + 4, :shard]


def finish(rep_at, pieces, n_exp):
    shard, lanes = pieces[0].shape
    vmem = pl.BlockSpec(memory_space=pltpu.VMEM)
    return pl.pallas_call(
        finish_kernel,
        in_specs=[pl.BlockSpec(memory_space=pltpu.SMEM)] + [vmem] * 4,
        out_specs=[vmem] * 3,
        out_shape=[
            jax.ShapeDtypeStruct((shard, 4 * (lanes - LANES)), f32),
            jax.ShapeDtypeStruct((shard, n_exp), f32),
            jax.ShapeDtypeStruct((4, shard), f32),
        ],
        name="finish",
    )(rep_at.reshape(1), *pieces)


def experts_finish_kernel(
    pair_home, pair_got, pair_sent, down_home, down_got, down_sent, out_ref
):
    for j in range(out_ref.shape[2]):
        for g in range(2):
            out_ref[:, g, j, :] = (
                pair_home[0, j, g].astype(f32)
                + pair_got[0, j, g].astype(f32)
                + pair_sent[j, g].astype(f32)
            )
        out_ref[:, 2, j, :] = (
            down_home[0, j].astype(f32) + down_got[0, j].astype(f32) + down_sent[j].astype(f32)
        )


def experts_finish(pair_terms, down_terms):
    exp_dev, pairs, hidden, width = pair_terms[2].shape
    rows = 32
    pair_spec = pl.BlockSpec((1, exp_dev, pairs, rows, width), lambda i: (0, 0, 0, i, 0))
    down_spec = pl.BlockSpec((1, exp_dev, rows, width), lambda i: (0, 0, i, 0))
    out = pl.pallas_call(
        experts_finish_kernel,
        grid=(hidden // rows,),
        in_specs=[
            pair_spec,
            pair_spec,
            pl.BlockSpec((exp_dev, pairs, rows, width), lambda i: (0, 0, i, 0)),
            down_spec,
            down_spec,
            pl.BlockSpec((exp_dev, rows, width), lambda i: (0, i, 0)),
        ],
        out_specs=pl.BlockSpec((rows, 3, exp_dev, width), lambda i: (i, 0, 0, 0)),
        out_shape=jax.ShapeDtypeStruct((hidden, 3, exp_dev, width), f32),
        compiler_params=params(1),
        cost_estimate=cost(hidden * width * 18, hidden * width * 60),
        name="experts_finish",
    )(*pair_terms, *down_terms)
    return out.transpose(0, 2, 1, 3)


def turn_tables(seg, block_len):
    groups, rows = seg.shape
    at = jnp.arange(rows, dtype=jnp.int32)
    same_block = (at[:, None] // block_len) == (at[None, :] // block_len)
    mine = seg[:, :, None]
    theirs = seg[:, None, :]
    earlier = jnp.sum(((theirs < mine) & same_block).astype(jnp.int32), axis=-1)
    position = (at % block_len - earlier).astype(f32)
    frequency = jnp.power(rope_base, -jnp.arange(HEAD_DIM // 2, dtype=f32) * 2.0 / HEAD_DIM)
    angles = position.reshape(-1, 1) * frequency
    cosine = jnp.cos(angles)
    sine = jnp.sin(angles)
    allowed = (mine == theirs) & same_block & (at[:, None] >= at[None, :])
    return (
        jnp.concatenate([cosine, cosine], axis=1),
        jnp.concatenate([-sine, sine], axis=1),
        allowed.astype(f32).reshape(groups * rows, rows),
    )


def layer(tokens, out_grad, w_qkv, w_out, router, gains, experts, seg_ids, routes):
    block_len = seg_ids.shape[1]
    rows_dev, width = tokens.shape
    n_exp = router.shape[1]
    exp_dev = experts.shape[1]
    top_count = routes.shape[1]
    n_fsdp = lax.axis_size("fsdp")
    rep_at = lax.axis_index("rep")
    fsdp_at = lax.axis_index("fsdp")
    capacity = max(2, block_len * top_count * 5 // (4 * n_exp))
    shard = w_qkv.shape[0]
    part = width // 4

    small = jnp.concatenate([router, gains.T, jnp.zeros((shard, LANES - n_exp - 4), bf16)], axis=1)
    pieces = pack(rep_at, w_qkv, small)
    pieces = [pieces[0]] + [hop(pieces[q], q) for q in range(1, 4)]
    chunk = chunk_of(rep_at, pieces, w_out)
    w_full, marks = fsdp_gather(chunk, axis=1)
    w_full = w_full.reshape(width, 4 * part + LANES)

    tok_ext = jnp.concatenate(
        [tokens, jnp.pad(seg_ids.reshape(rows_dev, 1), ((0, 0), (0, LANES - 1))).astype(bf16)],
        axis=1,
    )
    tok_parts = rep_gather(tok_ext)
    seg_all = jnp.stack([item[:, width].astype(jnp.int32) for item in tok_parts])
    tables = turn_tables(seg_all, block_len)

    e_own = lax.optimization_barrier(after(experts, chunk).transpose(1, 2, 0, 3))
    pair_far = far(after(e_own[:, 0:2], tok_parts[2]))
    e_near = near(e_own)
    pair_corner = near(pair_far)

    g_ext = jnp.concatenate(
        [out_grad, jnp.pad(routes, ((0, 0), (0, LANES - top_count))).astype(bf16)], axis=1
    )
    g_all = lax.all_gather(after(g_ext, *marks), "fsdp", axis=0, tiled=True)

    w_full = after(w_full, *tables)
    gain_f = w_full[:, 4 * part + n_exp : 4 * part + n_exp + 4].astype(f32).T
    normed_all, qkv, square_sums = qkv_rows(tok_parts, gain_f, w_full)
    sums = [square_sums] + [hop(square_sums, q) for q in range(1, 4)]
    mixed_rows, near_parts, home_parts = attn(rep_at, qkv, sums, gain_f, tables, w_full)
    terms = rep_sum(near_parts, home_parts)
    hidden, normed2 = middle(tokens, terms, gain_f)
    down_far = far(after(e_own[:, 2:3], normed2))
    down_corner = near(down_far)
    e_parts = (e_own, e_near, pair_far, down_far, pair_corner, down_corner)

    n2_all, _ = fsdp_gather(after(normed2, g_all))
    n2_all = n2_all.reshape(n_fsdp * rows_dev, width)
    rows_in, rows_up, aux = dispatch(
        fsdp_at, n2_all, g_all, w_full, n_exp, exp_dev, capacity, block_len
    )
    slot_shape = rows_in.shape
    rows_in = rows_in.reshape(exp_dev, -1, width)
    rows_up = rows_up.reshape(exp_dev, -1, width)
    produced, rows_grad, active, bars = ffn(rows_in, rows_up, e_parts)
    back_part, mix_part = combine(
        fsdp_at,
        produced.reshape(slot_shape),
        rows_grad.reshape(slot_shape),
        aux,
        g_all,
        n_exp,
        block_len,
    )
    near_pair, near_down, home_pair, home_down = ffn_grad(rows_in, rows_up, active, bars)
    back_got = fsdp_scatter_sum(back_part.reshape(n_fsdp, rows_dev, -1))
    mix_got = lax.psum_scatter(after(mix_part, back_got), "fsdp", scatter_dimension=0, tiled=True)
    down_terms = rep_sum(near_down, home_down)

    hidden_grad, attn_grad, gain_three, router_part = middle_back(
        back_got, hidden, normed2, out_grad, w_full, gain_f, n_exp
    )
    grads, inner, gain_mid, attn_all = attn_back(
        rep_at, rep_gather(attn_grad), qkv, sums, gain_f, tables, w_full
    )
    inners = [inner] + [hop(inner, q) for q in range(1, 4)]
    qkv_grad, near_parts, home_parts, gain_zero = heads_back(
        rep_at, grads, qkv, sums, inners, gain_f, tok_parts, w_full
    )
    home, got, sent = rep_sum(near_parts, home_parts)

    w_grad = weight_grad(
        rep_at,
        normed_all,
        qkv_grad,
        mixed_rows,
        attn_all,
        router_part,
        gain_zero,
        gain_mid,
        gain_three,
        n_exp,
        (n_fsdp, shard),
    )
    layer_out = (hidden + mix_got.astype(f32)).astype(bf16)

    pair_home, pair_got, pair_sent = rep_sum(near_pair, home_pair)
    w_got = fsdp_scatter_sum(w_grad, axis=1, hold=(mix_got,))

    expert_grad = experts_finish((pair_home, pair_got, pair_sent), down_terms)
    normed_grad = home[0] + got[0].astype(f32) + sent.astype(f32)
    inputs = tokens.astype(f32)
    tokens_grad = hidden_grad + norm_back(inputs, rms_scale(inputs), gain_f[0], normed_grad)
    w_got = after(w_got, expert_grad, tokens_grad, layer_out)
    grad_wout, *pieces = unpack(rep_at, w_got)
    pieces = [pieces[0]] + [hop(pieces[q], q) for q in range(1, 4)]
    grad_qkv, grad_router, grad_gains = finish(rep_at, pieces, n_exp)
    return layer_out, tokens_grad, grad_qkv, grad_wout, grad_router, grad_gains, expert_grad


def solution(mesh):
    in_specs = (
        P(("rep", "fsdp"), None),
        P(("rep", "fsdp"), None),
        P(("rep", "fsdp"), None),
        P(("rep", "fsdp"), None),
        P(("rep", "fsdp"), None),
        P(None, ("rep", "fsdp")),
        P("rep", "fsdp", None, None),
        P(("rep", "fsdp"), None),
        P(("rep", "fsdp"), None),
    )
    out_specs = (
        P(("rep", "fsdp"), None),
        P(("rep", "fsdp"), None),
        P(("rep", "fsdp"), None),
        P(("rep", "fsdp"), None),
        P(("rep", "fsdp"), None),
        P(None, ("rep", "fsdp")),
        P("rep", "fsdp", None, None),
    )
    return jax.shard_map(layer, mesh=mesh, in_specs=in_specs, out_specs=out_specs, check_vma=False)
```
